128 devices in a mesh: prow: 8 (over x, z_lo), pcol: 16 (over y, z_hi, core).
Axes of the slice: x: 4, y: 4, z: 4 (z_hi: 2, z_lo: 2; z = z_hi * 2 + z_lo), core: 2. Of those that a mesh axis runs over, the one named last changes fastest.
Arguments:
- inverse_matrix: float32 [24576, 24576], P('prow', 'pcol'), may hold values from -6 to 6
- factor_blocks: float32 [4, 96, 256, 256], P(None, 'prow', 'pcol'), may hold values from -0.0390625 to 0.0390625
- factor_inverse: float32 [4, 256, 256], replicated, may hold values from -8 to 8, as said below
- diag_given: float32 [4, 256, 256], replicated, may hold values from -6 to 6
- block_lists: int32 [4, 96], replicated, may hold values from 0 to 95, as said below
- list_mask: int32 [4, 96], replicated, may hold values from 0 to 1, as said below
- slot_of_block: int32 [96], replicated, may hold values from 0 to 95, as said below
Outputs:
- panel_inverse: float32 [4, 96, 256, 256], P(None, 'prow', 'pcol')
- diag_inverse: float32 [4, 256, 256], replicated
The draws below stay inside these ranges and needn't reach their ends.
Inputs may be any that keep to these rules, and one draw needn't show every extreme that they name: `block_lists`: each panel's list names every block of the window once; entries with mask 0 are padding. `list_mask`: 1 marks a used list entry; for every k, of the 48 pairs (p, s) with s // 12 = k, exactly 36 have slot_valid[p, s] = 1. `slot_of_block`: a permutation of the 96 slots. `factor_inverse`: lower triangular with a positive diagonal.
All inputs are finite; a program needn't handle non-finite values.
Results may differ from the reference program's by a relative error of at most 0.00007.
Values sent between devices are 32-bit elements; how exact they have to be, the bound alone decides.
A program may use at most 128 MiB of HBM per device.

```python
import math
import jax
import jax.numpy as jnp
from jax import lax

B = 256
P_SIZE = 4
NB = 96
RBLK = 12
KEEP = 36


def draw_factor_inverse(key, part):
    key_diag = jax.random.fold_in(key, 11)
    key_lower = jax.random.fold_in(key, 12)
    diagonal = jnp.exp(jax.random.uniform(key_diag, (P_SIZE, B), jnp.float32, math.log(0.5), math.log(2.0)))
    lower_part = jnp.clip(jax.random.normal(key_lower, (P_SIZE, B, B), jnp.float32), -4.0, 4.0) / math.sqrt(B)
    identity = jnp.eye(B, dtype=jnp.float32)
    return jnp.tril(lower_part, -1) + diagonal[:, :, None] * identity[None, :, :]


def window_lists(key):
    key_slots = jax.random.fold_in(key, 21)
    key_lists = jax.random.fold_in(key, 22)
    key_valid = jax.random.fold_in(key, 23)
    slot_table = jax.random.permutation(key_slots, jnp.arange(NB, dtype=jnp.int32)).astype(jnp.int32)
    list_keys = jax.random.split(key_lists, P_SIZE)
    lists = jax.vmap(lambda one: jax.random.permutation(one, jnp.arange(NB, dtype=jnp.int32)))(list_keys).astype(jnp.int32)
    group_keys = jax.random.split(key_valid, NB // RBLK)
    ranks = jax.vmap(lambda one: jax.random.permutation(one, jnp.arange(P_SIZE * RBLK, dtype=jnp.int32)))(group_keys)
    used = (ranks < KEEP).astype(jnp.int32).reshape(NB // RBLK, P_SIZE, RBLK)
    used = jnp.transpose(used, (1, 0, 2)).reshape(P_SIZE, NB)
    slots = slot_table[lists]
    masks = jnp.take_along_axis(used, slots, axis=1).astype(jnp.int32)
    return (lists, masks, slot_table)


def draw_block_lists(key, part):
    return window_lists(key)[0]


def draw_list_mask(key, part):
    return window_lists(key)[1]


def draw_slot_of_block(key, part):
    return window_lists(key)[2]


def steps_of(stream_key, extent, shards, low, top_value):
    def one(axis_at, parts):
        draws = jax.random.uniform(jax.random.fold_in(jax.random.fold_in(stream_key, 6), axis_at), (parts,), jnp.float32, low / len(shards), top_value / len(shards))
        return jnp.repeat(jnp.exp(draws), extent[axis_at] // parts).reshape((-1,) + (1,) * (len(extent) - axis_at - 1))

    gain = one(*shards[0])
    for cut in shards[1:]:
        gain = gain * one(*cut)
    return gain


def bell_draw(stream_key, dims, scale, reach, cuts=(), held_as=jnp.bfloat16):
    loudness = steps_of(stream_key, dims, cuts, -0.22, 0.18) if cuts else 1.0
    entries = jax.random.normal(stream_key, dims, jnp.float32) * scale * loudness
    return jnp.minimum(jnp.maximum(entries, -reach), reach).astype(held_as)


def setup_inputs(seed: int = 0) -> dict:
    keys = jax.random.split(jax.random.key(seed), 8)
    return {
        "inverse_matrix": bell_draw(keys[0], (NB * B, NB * B), 1.0, 6.0, ((0, 8), (1, 16)), jnp.float32),
        "factor_blocks": bell_draw(keys[1], (P_SIZE, NB, B, B), ((NB * B) ** -0.5), 0.0390625, ((1, 8), (2, 16)), jnp.float32),
        "factor_inverse": draw_factor_inverse(jax.random.fold_in(keys[7], 71), 0),
        "diag_given": bell_draw(keys[3], (P_SIZE, B, B), 1.0, 6.0, (), jnp.float32),
        "block_lists": draw_block_lists(jax.random.fold_in(keys[7], 71), 0),
        "list_mask": draw_list_mask(jax.random.fold_in(keys[7], 71), 0),
        "slot_of_block": draw_slot_of_block(jax.random.fold_in(keys[7], 71), 0),
    }


def valid_slots(block_lists, list_mask, slot_of_block):
    window_blocks = block_lists.shape[1]
    block_ids = jnp.arange(window_blocks, dtype=jnp.int32)
    chosen = (block_lists[:, :, None] == block_ids[None, None, :]).astype(jnp.int32)
    slot_ids = jnp.sum(chosen * slot_of_block[None, None, :], axis=2).astype(jnp.int32)
    matches = (slot_ids[:, :, None] == block_ids[None, None, :]).astype(jnp.int32) * list_mask[:, :, None]
    return jnp.sum(matches, axis=1).astype(jnp.int32)


def reference(inverse_matrix, factor_blocks, factor_inverse, diag_given, block_lists, list_mask, slot_of_block):
    highest = lax.Precision.HIGHEST
    slot_valid = valid_slots(block_lists, list_mask, slot_of_block).astype(jnp.float32)
    normalized = jnp.einsum("psij,pjk->psik", factor_blocks, factor_inverse, precision=highest)
    normalized = normalized * slot_valid[:, :, None, None]
    panel_width = factor_inverse.shape[1]
    window_blocks = block_lists.shape[1]

    def one_panel(operands):
        normal_hat, valid_rows = operands
        column_stack = normal_hat.reshape(window_blocks * panel_width, panel_width)
        product = jnp.dot(inverse_matrix, column_stack, precision=highest, preferred_element_type=jnp.float32)
        return -(product.reshape(window_blocks, panel_width, panel_width) * valid_rows[:, None, None])

    panel_inverse = lax.map(one_panel, (normalized, slot_valid))
    diag_inverse = diag_given - jnp.einsum("psik,psil->pkl", normalized, panel_inverse, precision=highest)
    return panel_inverse, diag_inverse
```

```python
import functools

import jax
import jax.numpy as jnp
from jax import lax
from jax.experimental import pallas as pl
from jax.experimental.pallas import tpu as pltpu
from jax.sharding import PartitionSpec as P

MESH = pl.DeviceIdType.MESH
F32 = jnp.float32
BF16 = jnp.bfloat16
KEEP = 36
HALF_A = 16
NEED = 24
QR = 3


def coords():
    k = lax.axis_index("prow")
    j = lax.axis_index("pcol")
    return k // 2, j // 4, (j // 2) % 2, k % 2, j % 2


def dev(x, y, zh, zl, c):
    return (x * 2 + zl, (y * 2 + zh) * 2 + c)


def split2(v):
    hi = v.astype(BF16)
    lo = (v - hi.astype(F32)).astype(BF16)
    return hi, lo


def dot3(ah, al, bh, bl):
    out = jnp.dot(ah, bh, preferred_element_type=F32)
    out += jnp.dot(ah, bl, preferred_element_type=F32)
    out += jnp.dot(al, bh, preferred_element_type=F32)
    return out


def valid_slots(block_lists, list_mask, slot_of_block):
    window_blocks = block_lists.shape[1]
    block_ids = jnp.arange(window_blocks, dtype=jnp.int32)
    chosen = (block_lists[:, :, None] == block_ids[None, None, :]).astype(jnp.int32)
    slot_ids = jnp.sum(chosen * slot_of_block[None, None, :], axis=2)
    matches = (slot_ids[:, :, None] == block_ids[None, None, :]).astype(jnp.int32) * list_mask[
        :, :, None
    ]
    return jnp.sum(matches, axis=1)


def packed_order(valid, group):
    v = lax.dynamic_slice_in_dim(valid, group * 12, 12, 1)
    v = v.reshape(4, 2, 6).transpose(1, 0, 2).reshape(48)
    i = jnp.arange(48, dtype=jnp.int32)
    pos = jnp.sum(v[None, :] * (i[None, :] < i[:, None]).astype(jnp.int32), axis=1)
    q = jnp.arange(KEEP, dtype=jnp.int32)
    hit = (pos[None, :] == q[:, None]).astype(jnp.int32) * v[None, :]
    idx = jnp.sum(hit * i[None, :], axis=1)
    return jnp.where(v > 0, pos, -1), idx


def prep_kernel(tab, f_ref, inv_ref, nc_ref, nd_ref):
    for p in range(4):
        nd_ref[p] = jnp.dot(
            f_ref[p].reshape(192, 256),
            inv_ref[p],
            precision=lax.Precision.HIGHEST,
            preferred_element_type=F32,
        ).reshape(12, 16, 256)

    @pl.loop(0, KEEP)
    def _(q):
        nc_ref[q] = nd_ref[tab[1, q], tab[0, q]]


def main_kernel(
    tab, g_hbm, nc, out, ghi, glo, stage, ng, nhi, nlo, pb, rc, ra, rb, rp, rm, rz,
    g_sem, p1_s, p1_r, xp_s, xp_r, xm_s, xm_r, z_s, z_r, c_s, c_r, rs_s, rs_r,
):
    x, y, zh, zl, c = coords()
    xp, xm, xf = (x + 1) % 4, (x + 3) % 4, (x + 2) % 4
    yp, ym, yf = (y + 1) % 4, (y + 3) % 4, (y + 2) % 4
    zn = 1 - zl
    d_xp, d_xm = dev(xp, y, zh, zl, c), dev(xm, y, zh, zl, c)
    d_zn, d_c = dev(x, y, zh, zn, c), dev(x, y, zh, zl, 1 - c)
    d_yp, d_ym = dev(x, yp, zh, zl, c), dev(x, ym, zh, zl, c)
    d_z2 = dev(x, y, 1 - zh, zl, c)
    d_to = dev((x + y) % 4, x, zl, zh, c)
    d_from = dev(y, (x + 4 - y) % 4, zl, zh, c)
    own_target = ((x == 0) & (y == 0)) & (zl == zh)

    barrier = pltpu.get_barrier_semaphore()
    for d in (d_xp, d_xm, d_zn, d_c, d_yp, d_ym, d_z2):
        pl.semaphore_signal(barrier, inc=1, device_id=d, device_id_type=MESH)

    @pl.when(jnp.logical_not(own_target))
    def _():
        for d in (d_to, d_from):
            pl.semaphore_signal(barrier, inc=1, device_id=d, device_id_type=MESH)
        pl.semaphore_wait(barrier, 9)

    @pl.when(own_target)
    def _():
        pl.semaphore_wait(barrier, 7)

    def share(xx, z):
        return 2 * (2 * ((xx + 4 - y) % 4) + z) + c

    r_me = (y * 2 + zh) * 2 + c
    s_o, s_l, s_r, s_f = (share(v, zl) for v in (x, xm, xp, xf))
    t_o, t_l, t_r, t_f = (share(v, zn) for v in (x, xm, xp, xf))
    a0, a1, a2 = 0, HALF_A // 2, HALF_A
    b1, b2 = (HALF_A + KEEP) // 2, KEEP

    def rcopy(src, dst, ss, rs, d):
        return pltpu.make_async_remote_copy(
            src_ref=src, dst_ref=dst, send_sem=ss, recv_sem=rs, device_id=d, device_id_type=MESH
        )

    def piece(lo, hi, s):
        return ng.at[pl.ds(lo, hi - lo), s]

    spans = ((a0, a2), (a2, b2))

    def p1(i):
        lo, hi = spans[i]
        return rcopy(nc.at[pl.ds(lo, hi - lo)], piece(lo, hi, r_me), p1_s.at[i], p1_r.at[i], d_to)

    def p1_local(i):
        lo, hi = spans[i]
        return pltpu.make_async_copy(nc.at[pl.ds(lo, hi - lo)], piece(lo, hi, s_o), p1_r.at[i])

    @pl.when(jnp.logical_not(own_target))
    def _():
        p1(0).start()
        p1(1).start()

    @pl.when(own_target)
    def _():
        p1_local(0).start()
        p1_local(1).start()

    def g_copy(i, slot):
        return pltpu.make_async_copy(
            g_hbm.at[pl.ds(i * 256, 256), :], stage.at[slot], g_sem.at[slot]
        )

    g_copy(0, 0).start()

    def load_g(i, carry):
        slot = i % 2
        g_copy(i, slot).wait()

        @pl.when(i < 11)
        def _():
            g_copy(i + 1, 1 - slot).start()

        for r in range(0, 256, 64):
            hi, lo = split2(stage[slot, r : r + 64, :])
            ghi[i, r : r + 64, :] = hi
            glo[i, r : r + 64, :] = lo
        return carry

    lax.fori_loop(0, 12, load_g, 0)

    to_xp = (
        (a0, a2, s_o), (a2, b2, s_o), (a2, b2, t_o), (a0, a1, s_l), (a2, b1, s_l), (a2, b1, t_l),
    )
    to_xm = (
        (a0, a2, s_o), (a2, b2, s_o), (a2, b2, t_o), (a1, a2, s_r), (b1, b2, s_r), (b1, b2, t_r),
    )
    to_z = ((a0, a2, s_o), (a2, b2, s_o), (a0, a2, s_l), (a0, a2, s_r), (a0, a1, s_f), (a1, a2, s_f))
    of_xm = (
        (a0, a2, s_l), (a2, b2, s_l), (a2, b2, t_l), (a0, a1, s_f), (a2, b1, s_f), (a2, b1, t_f),
    )
    of_xp = (
        (a0, a2, s_r), (a2, b2, s_r), (a2, b2, t_r), (a1, a2, s_f), (b1, b2, s_f), (b1, b2, t_f),
    )
    of_z = ((a0, a2, t_o), (a2, b2, t_o), (a0, a2, t_l), (a0, a2, t_r), (a0, a1, t_f), (a1, a2, t_f))

    def go(table, sems, d, i):
        lo, hi, s = table[i]
        return rcopy(piece(lo, hi, s), piece(lo, hi, s), sems[0].at[i], sems[1].at[i], d)

    xps, xms, zs = (xp_s, xp_r), (xm_s, xm_r), (z_s, z_r)

    def send_xp(i):
        go(to_xp, xps, d_xp, i).start()

    def send_xm(i):
        go(to_xm, xms, d_xm, i).start()

    def send_z(i):
        go(to_z, zs, d_zn, i).start()

    def got_xm(i):
        go(of_xm, xps, d_xp, i).wait_recv()

    def got_xp(i):
        go(of_xp, xms, d_xm, i).wait_recv()

    def got_z(i):
        go(of_z, zs, d_zn, i).wait_recv()

    def twin(i, s, mine):
        first = (1 - c if mine else c) * (KEEP - NEED)
        return rcopy(
            ng.at[pl.ds(first, NEED), s], ng.at[pl.ds(first, NEED), s], c_s.at[i], c_r.at[i], d_c
        )

    order = (s_o, s_l, s_r, t_o, s_f, t_l, t_r, t_f)

    def send_c(i):
        twin(i, order[i], True).start()

    @pl.when(jnp.logical_not(own_target))
    def _():
        p1(0).wait_recv()

    @pl.when(own_target)
    def _():
        p1_local(0).wait()

    send_xp(0)
    send_xm(0)
    send_z(0)

    @pl.when(jnp.logical_not(own_target))
    def _():
        p1(1).wait_recv()

    @pl.when(own_target)
    def _():
        p1_local(1).wait()

    send_xp(1)
    send_xm(1)
    send_z(1)
    send_c(0)
    got_xm(0)
    send_xp(3)
    send_z(2)
    got_xp(0)
    send_xm(3)
    send_z(3)
    got_xm(1)
    send_xp(4)
    send_c(1)
    got_xp(1)
    send_xm(4)
    send_c(2)
    got_z(0)
    got_z(1)
    send_xp(2)
    send_xm(2)
    send_c(3)
    got_xm(3)
    send_z(4)
    got_xp(3)
    send_z(5)
    got_xm(2)
    send_xp(5)
    got_xp(2)
    send_xm(5)
    got_xm(4)
    got_xp(4)
    send_c(4)
    got_z(2)
    send_c(5)
    got_z(3)
    send_c(6)
    got_xm(5)
    got_xp(5)
    got_z(4)
    got_z(5)
    send_c(7)
    for i in range(8):
        twin(i, order[i] + 1 - 2 * c, False).wait_recv()

    def spread(i, carry):
        p, t = i // 6, i % 6
        at = tab[2, i]
        used = at >= 0
        block = jnp.where(used, ng[jnp.maximum(at, 0)].reshape(256, 256), 0.0)
        hi, lo = split2(block)
        nhi[p, t] = hi
        nlo[p, t] = lo
        return carry

    lax.fori_loop(0, 24, spread, 0)

    rounds = KEEP // QR

    def product(q):
        s, p = tab[0, q], tab[1, q]
        bh = nhi[p].reshape(1536, 256)
        bl = nlo[p].reshape(1536, 256)
        pb[q] = dot3(ghi[s], glo[s], bh, bl).reshape(4, 2, 2, 16, 256)

    def m_core(g, mine):
        qs = pl.ds(g * QR, QR)
        return rcopy(pb.at[qs, :, :, 1 - c], rc.at[qs], rs_s.at[0, g], rs_r.at[0, g], d_c)

    def m_a(g):
        qs = pl.ds(g * QR, QR)
        return rcopy(pb.at[qs, yf, 0, c], ra.at[qs], rs_s.at[1, g], rs_r.at[1, g], d_yp)

    def m_b(g):
        qs = pl.ds(g * QR, QR)
        return rcopy(pb.at[qs, yf, 1, c], rb.at[qs], rs_s.at[2, g], rs_r.at[2, g], d_ym)

    def m_p(g):
        qs = pl.ds(g * QR, QR)
        return rcopy(pb.at[qs, yp, :, c], rp.at[qs], rs_s.at[3, g], rs_r.at[3, g], d_yp)

    def m_m(g):
        qs = pl.ds(g * QR, QR)
        return rcopy(pb.at[qs, ym, :, c], rm.at[qs], rs_s.at[4, g], rs_r.at[4, g], d_ym)

    def m_z(g):
        qs = pl.ds(g * QR, QR)
        return rcopy(pb.at[qs, y, 1 - zh, c], rz.at[qs], rs_s.at[5, g], rs_r.at[5, g], d_z2)

    def step(i, carry):
        @pl.when(i < rounds)
        def _():
            @pl.loop(0, QR)
            def _(n):
                product(i * QR + n)

            m_core(i, True).start()

        @pl.when((i >= 1) & (i < rounds + 1))
        def _():
            g = i - 1
            m_core(g, False).wait_recv()

            @pl.loop(0, QR)
            def _(n):
                q = g * QR + n
                pb[q, :, :, c] += rc[q]

            m_a(g).start()
            m_b(g).start()

        @pl.when((i >= 2) & (i < rounds + 2))
        def _():
            g = i - 2
            m_a(g).wait_recv()
            m_b(g).wait_recv()

            @pl.loop(0, QR)
            def _(n):
                q = g * QR + n
                pb[q, yp, 0, c] += ra[q]
                pb[q, ym, 1, c] += rb[q]

            m_p(g).start()
            m_m(g).start()

        @pl.when((i >= 3) & (i < rounds + 3))
        def _():
            g = i - 3
            m_p(g).wait_recv()
            m_m(g).wait_recv()

            @pl.loop(0, QR)
            def _(n):
                q = g * QR + n
                pb[q, y, :, c] += rp[q] + rm[q]

            m_z(g).start()

        @pl.when(i >= 4)
        def _():
            g = i - 4
            m_z(g).wait_recv()

            @pl.loop(0, QR)
            def _(n):
                q = g * QR + n
                out[q] = -(pb[q, y, zh, c] + rz[q])

        return carry

    lax.fori_loop(0, rounds + 4, step, 0)

    @pl.when(jnp.logical_not(own_target))
    def _():
        p1(0).wait_send()
        p1(1).wait_send()

    for i in range(6):
        go(to_xp, xps, d_xp, i).wait_send()
        go(to_xm, xms, d_xm, i).wait_send()
        go(to_z, zs, d_zn, i).wait_send()
    for i in range(8):
        twin(i, order[i], True).wait_send()

    @pl.loop(0, rounds)
    def _(g):
        m_core(g, True).wait_send()
        m_a(g).wait_send()
        m_b(g).wait_send()
        m_p(g).wait_send()
        m_m(g).wait_send()
        m_z(g).wait_send()


def tail_kernel(tab, pi_ref, nd_ref, out_ref, d_ref):
    for p in range(4):
        for s in range(12):
            at = tab[3, (s // 6) * 24 + p * 6 + s % 6]
            out_ref[p, s] = jnp.where(at >= 0, pi_ref[jnp.maximum(at, 0)], 0.0)
    for p in range(4):
        d_ref[p] = lax.dot_general(
            nd_ref[p].reshape(192, 256),
            out_ref[p].reshape(192, 256),
            (((0,), (0,)), ((), ())),
            precision=lax.Precision.HIGHEST,
            preferred_element_type=F32,
        )


def sum_kernel(d_ref, out, work, r0, r1, r2, r3, s_sem, r_sem):
    x, y, zh, zl, c = coords()
    z = 2 * zh + zl
    first = jnp.where(c == 0, x, y)
    second = jnp.where(c == 0, y, x)

    def peer(axis, step):
        if axis == 0:
            a, b, e = (first + step) % 4, second, z
        elif axis == 1:
            a, b, e = first, (second + step) % 4, z
        else:
            a, b, e = first, second, (z + step) % 4
        xx, yy = jnp.where(c == 0, a, b), jnp.where(c == 0, b, a)
        return dev(xx, yy, e // 2, e % 2, c)

    twin = dev(x, y, zh, zl, 1 - c)
    barrier = pltpu.get_barrier_semaphore()
    pl.semaphore_signal(barrier, inc=1, device_id=twin, device_id_type=MESH)
    for axis in range(3):
        for step in (1, 2, 3):
            pl.semaphore_signal(barrier, inc=1, device_id=peer(axis, step), device_id_type=MESH)
    pl.semaphore_wait(barrier, 10)

    def rcopy(src, dst, i, d):
        return pltpu.make_async_remote_copy(
            src_ref=src, dst_ref=dst, send_sem=s_sem.at[i], recv_sem=r_sem.at[i],
            device_id=d, device_id_type=MESH,
        )

    pending = []
    cp = rcopy(d_ref.at[1 - c], r0, 0, twin)
    cp.start()
    cp.wait_recv()
    pending.append(cp)
    work[...] = d_ref[c] + r0[...]
    at = (first, second, z)
    recv = (r1, r2, r3)
    n = 1
    for axis in range(3):
        view = work
        for a in range(axis):
            view = view.at[at[a]]
        cps = []
        for step in (1, 3, 2):
            cp = rcopy(view.at[(at[axis] + step) % 4], recv[axis].at[step - 1], n, peer(axis, step))
            n += 1
            cp.start()
            cps.append(cp)
        for cp in cps:
            cp.wait_recv()
        pending += cps
        mine = view.at[at[axis]]
        mine[...] = mine[...] + (recv[axis][0] + recv[axis][1] + recv[axis][2])
    me = out.at[c, at[0], at[1], at[2]]
    me[...] = work[at[0], at[1], at[2]]
    for axis in (2, 1, 0):
        part = out.at[c]
        for a in range(axis + 1):
            part = part.at[at[a]]
        cps = []
        for step in (1, 3, 2):
            cp = rcopy(part, part, n, peer(axis, step))
            n += 1
            cp.start()
            cps.append(cp)
        for cp in cps:
            cp.wait_recv()
        pending += cps
    cp = rcopy(out.at[c], out.at[c], n, twin)
    cp.start()
    cp.wait_recv()
    pending.append(cp)
    for cp in pending:
        cp.wait_send()


VM = pl.BlockSpec(memory_space=pltpu.VMEM)
SM = pl.BlockSpec(memory_space=pltpu.SMEM)
ANY = pl.BlockSpec(memory_space=pl.ANY)
DMA = pltpu.SemaphoreType.DMA


def on_device(
    inverse_matrix, factor_blocks, factor_inverse, diag_given, block_lists, list_mask, slot_of_block
):
    k = lax.axis_index("prow")
    j = lax.axis_index("pcol")
    valid = valid_slots(block_lists, list_mask, slot_of_block)
    pos_row, idx = packed_order(valid, k)
    pos_col, _ = packed_order(valid, j // 2)
    s_q = (idx // 24) * 6 + idx % 6
    p_q = (idx % 24) // 6
    col = lax.dynamic_slice_in_dim(pos_col, (j % 2) * 24, 24, 0)
    tab = jnp.stack(
        [jnp.pad(s_q, (0, 12)), jnp.pad(p_q, (0, 12)), jnp.pad(col, (0, 24)), pos_row]
    )

    nc, nd = pl.pallas_call(
        prep_kernel,
        out_shape=(
            jax.ShapeDtypeStruct((KEEP, 16, 256), F32),
            jax.ShapeDtypeStruct((4, 12, 16, 256), F32),
        ),
        in_specs=[SM, VM, VM],
        out_specs=(VM, VM),
        name="normalize",
    )(tab, factor_blocks, factor_inverse)

    rounds = KEEP // QR
    pi = pl.pallas_call(
        main_kernel,
        out_shape=jax.ShapeDtypeStruct((KEEP, 16, 256), F32),
        in_specs=[SM, ANY, VM],
        out_specs=VM,
        scratch_shapes=[
            pltpu.VMEM((12, 256, 1536), BF16),
            pltpu.VMEM((12, 256, 1536), BF16),
            pltpu.VMEM((2, 256, 1536), F32),
            pltpu.VMEM((KEEP, 16, 16, 256), F32),
            pltpu.VMEM((4, 6, 256, 256), BF16),
            pltpu.VMEM((4, 6, 256, 256), BF16),
            pltpu.VMEM((KEEP, 4, 2, 2, 16, 256), F32),
            pltpu.VMEM((KEEP, 4, 2, 16, 256), F32),
            pltpu.VMEM((KEEP, 16, 256), F32),
            pltpu.VMEM((KEEP, 16, 256), F32),
            pltpu.VMEM((KEEP, 2, 16, 256), F32),
            pltpu.VMEM((KEEP, 2, 16, 256), F32),
            pltpu.VMEM((KEEP, 16, 256), F32),
            DMA((2,)),
            DMA((2,)),
            DMA((2,)),
            DMA((6,)),
            DMA((6,)),
            DMA((6,)),
            DMA((6,)),
            DMA((6,)),
            DMA((6,)),
            DMA((8,)),
            DMA((8,)),
            DMA((6, rounds)),
            DMA((6, rounds)),
        ],
        compiler_params=pltpu.CompilerParams(
            collective_id=0, has_side_effects=True, vmem_limit_bytes=67043328
        ),
        name="window",
    )(tab, inverse_matrix, nc)

    panel_inverse, terms = pl.pallas_call(
        tail_kernel,
        out_shape=(
            jax.ShapeDtypeStruct((4, 12, 16, 256), F32),
            jax.ShapeDtypeStruct((4, 256, 256), F32),
        ),
        in_specs=[SM, VM, VM],
        out_specs=(VM, VM),
        name="unpack",
    )(tab, pi, nd)

    total = pl.pallas_call(
        sum_kernel,
        out_shape=jax.ShapeDtypeStruct((2, 4, 4, 4, 8, 256), F32),
        in_specs=[VM],
        out_specs=VM,
        scratch_shapes=[
            pltpu.VMEM((4, 4, 4, 8, 256), F32),
            pltpu.VMEM((4, 4, 4, 8, 256), F32),
            pltpu.VMEM((3, 4, 4, 8, 256), F32),
            pltpu.VMEM((3, 4, 8, 256), F32),
            pltpu.VMEM((3, 8, 256), F32),
            DMA((20,)),
            DMA((20,)),
        ],
        compiler_params=pltpu.CompilerParams(collective_id=1, has_side_effects=True),
        name="diag_sum",
    )(terms.reshape(2, 4, 4, 4, 8, 256))
    diag_inverse = diag_given - total.reshape(4, 256, 256)
    return (panel_inverse, diag_inverse)


def solution(mesh):
    return jax.shard_map(
        on_device,
        mesh=mesh,
        in_specs=(P("prow", "pcol"), P(None, "prow", "pcol", None), P(), P(), P(), P(), P()),
        out_specs=(P(None, "prow", "pcol", None), P()),
        check_vma=False,
    )
```

```python
import functools

import jax
import jax.numpy as jnp
from jax import lax
from jax.experimental import pallas as pl
from jax.experimental.pallas import tpu as pltpu
from jax.sharding import PartitionSpec as P

MESH = pl.DeviceIdType.MESH
F32 = jnp.float32
BF16 = jnp.bfloat16
KEEP = 36
FIRST = 24
QR = 3
STAGES = 4
ROWS = 128
LAGS = (1, 3, 5, 7)


def coords():
    k = lax.axis_index("prow")
    j = lax.axis_index("pcol")
    return k // 2, j // 4, (j // 2) % 2, k % 2, j % 2


def dev(x, y, zh, zl, c):
    return (x * 2 + zl, (y * 2 + zh) * 2 + c)


def split2(v):
    hi = v.astype(BF16)
    lo = (v - hi.astype(F32)).astype(BF16)
    return hi, lo


def valid_slots(block_lists, list_mask, slot_of_block):
    window_blocks = block_lists.shape[1]
    block_ids = jnp.arange(window_blocks, dtype=jnp.int32)
    chosen = (block_lists[:, :, None] == block_ids[None, None, :]).astype(jnp.int32)
    slot_ids = jnp.sum(chosen * slot_of_block[None, None, :], axis=2)
    matches = (slot_ids[:, :, None] == block_ids[None, None, :]).astype(jnp.int32) * list_mask[
        :, :, None
    ]
    return jnp.sum(matches, axis=1)


def packed_order(valid, group):
    v = lax.dynamic_slice_in_dim(valid, group * 12, 12, 1).reshape(48)
    i = jnp.arange(48, dtype=jnp.int32)
    pos = jnp.sum(v[None, :] * (i[None, :] < i[:, None]).astype(jnp.int32), axis=1)
    q = jnp.arange(KEEP, dtype=jnp.int32)
    hit = (pos[None, :] == q[:, None]).astype(jnp.int32) * v[None, :]
    idx = jnp.sum(hit * i[None, :], axis=1)
    return jnp.where(v > 0, pos, -1), idx


def prep_kernel(tab, f_ref, inv_ref, nc_ref, nd_ref):
    for p in range(4):
        nd_ref[p] = jnp.dot(
            f_ref[p].reshape(192, 256),
            inv_ref[p],
            precision=lax.Precision.HIGHEST,
            preferred_element_type=F32,
        ).reshape(12, 16, 256)

    @pl.loop(0, KEEP)
    def _(q):
        nc_ref[q] = nd_ref[tab[1, q], tab[0, q]]


def main_kernel(
    tab, g_hbm, nc, nd, given, pid, dout,
    out, ghi, glo, stage, ng0, ng1, nhi, nlo, pb, rc, ra, rb, rp, rm, rz, outx, ndt, pt, dw, e1, e2,
    g_sem, p1_s, p1_r, xp_s, xp_r, xm_s, xm_r, z_s, z_r, c_s, c_r, rs_s, rs_r, ar_s, ar_r,
):
    x, y, zh, zl, c = coords()
    z = 2 * zh + zl
    xp, xm, xf = (x + 1) % 4, (x + 3) % 4, (x + 2) % 4
    yp, ym, yf = (y + 1) % 4, (y + 3) % 4, (y + 2) % 4
    zn = 1 - zl
    d_xp, d_xm = dev(xp, y, zh, zl, c), dev(xm, y, zh, zl, c)
    d_zn, d_c = dev(x, y, zh, zn, c), dev(x, y, zh, zl, 1 - c)
    d_yp, d_ym = dev(x, yp, zh, zl, c), dev(x, ym, zh, zl, c)
    d_z2 = dev(x, y, 1 - zh, zl, c)
    d_to = dev((y + 2 * (x % 2)) % 4, x, zl, zh, c)
    d_from = dev(y, (x + 2 * (y % 2)) % 4, zl, zh, c)
    own_target = ((x == y) & (x % 2 == 0)) & (zl == zh)

    at = (jnp.where(c == 0, x, y), jnp.where(c == 0, y, x), z)

    def peer(n1, n2, n3):
        a, b, e = (at[0] + n1) % 4, (at[1] + n2) % 4, (at[2] + n3) % 4
        return dev(jnp.where(c == 0, a, b), jnp.where(c == 0, b, a), e // 2, e % 2, c)

    plane = [(n2, n3) for n2 in range(4) for n3 in range(4) if (n2, n3) != (0, 0)]

    barrier = pltpu.get_barrier_semaphore()
    for d in [d_c] + [peer(n, 0, 0) for n in (1, 2, 3)] + [peer(0, *n) for n in plane]:
        pl.semaphore_signal(barrier, inc=1, device_id=d, device_id_type=MESH)

    @pl.when(jnp.logical_not(own_target))
    def _():
        for d in (d_to, d_from):
            pl.semaphore_signal(barrier, inc=1, device_id=d, device_id_type=MESH)
        pl.semaphore_wait(barrier, 21)

    @pl.when(own_target)
    def _():
        pl.semaphore_wait(barrier, 19)

    def share(xx, zz):
        return 2 * (2 * ((xx + 2 * (y % 2)) % 4) + zz) + c

    r_me = (y * 2 + zh) * 2 + c
    s_o, s_l, s_r, s_f = (share(v, zl) for v in (x, xm, xp, xf))
    t_o, t_l, t_r, t_f = (share(v, zn) for v in (x, xm, xp, xf))
    cuts = ((0, 5, 10, 17, 24), (0, 3, 6, 9, 12))
    ng = (ng0, ng1)
    base = (0, FIRST)

    def rcopy(src, dst, ss, rs, d):
        return pltpu.make_async_remote_copy(
            src_ref=src, dst_ref=dst, send_sem=ss, recv_sem=rs, device_id=d, device_id_type=MESH
        )


    spans = tuple(((v[0], v[2]), (v[2], v[4])) for v in cuts)

    def p1(h, i):
        lo, hi = spans[h][i]
        return rcopy(
            nc.at[pl.ds(base[h] + lo, hi - lo)], ng[h].at[pl.ds(lo, hi - lo), r_me],
            p1_s.at[h, i], p1_r.at[h, i], d_to,
        )

    def p1_local(h, i):
        lo, hi = spans[h][i]
        return pltpu.make_async_copy(
            nc.at[pl.ds(base[h] + lo, hi - lo)], ng[h].at[pl.ds(lo, hi - lo), s_o], p1_r.at[h, i]
        )

    def m_rows():
        return rcopy(nd.at[pl.ds(2 * (1 - c), 2)], ndt, ar_s.at[0], ar_r.at[0], d_c)

    @pl.when(jnp.logical_not(own_target))
    def _():
        for h in (0, 1):
            for i in (0, 1):
                p1(h, i).start()

    @pl.when(own_target)
    def _():
        for h in (0, 1):
            for i in (0, 1):
                p1_local(h, i).start()

    def p1_wait(h, i):
        @pl.when(jnp.logical_not(own_target))
        def _():
            p1(h, i).wait_recv()

        @pl.when(own_target)
        def _():
            p1_local(h, i).wait()


    chunks = 3072 // ROWS

    def g_copy(i):
        slot = i % STAGES
        return pltpu.make_async_copy(
            g_hbm.at[pl.ds(i * ROWS, ROWS), :], stage.at[slot], g_sem.at[slot]
        )

    for n in range(STAGES - 1):
        g_copy(n).start()

    def load_g(i, carry):
        g_copy(i).wait()

        @pl.when(i < chunks - STAGES + 1)
        def _():
            g_copy(i + STAGES - 1).start()

        per = 256 // ROWS
        b, r0 = i // per, (i % per) * ROWS
        for r in range(0, ROWS, 64):
            hi, lo = split2(stage[i % STAGES, r : r + 64, :])
            at = pl.ds(pl.multiple_of(r0 + r, 64), 64)
            ghi[b, at, :] = hi
            glo[b, at, :] = lo
        return carry

    def some_g(lo, hi):
        lax.fori_loop(lo, hi, load_g, 0)


    to_xp = ((0, 2, s_o), (2, 4, s_o), (2, 4, t_o), (0, 1, s_l), (2, 3, s_l), (2, 3, t_l))
    to_xm = ((0, 2, s_o), (2, 4, s_o), (2, 4, t_o), (1, 2, s_r), (3, 4, s_r), (3, 4, t_r))
    to_z = ((0, 2, s_o), (2, 4, s_o), (0, 2, s_l), (0, 2, s_r), (0, 1, s_f), (1, 2, s_f))
    of_xm = ((0, 2, s_l), (2, 4, s_l), (2, 4, t_l), (0, 1, s_f), (2, 3, s_f), (2, 3, t_f))
    of_xp = ((0, 2, s_r), (2, 4, s_r), (2, 4, t_r), (1, 2, s_f), (3, 4, s_f), (3, 4, t_f))
    of_z = ((0, 2, t_o), (2, 4, t_o), (0, 2, t_l), (0, 2, t_r), (0, 1, t_f), (1, 2, t_f))
    order = (s_o, s_l, s_r, t_o, s_f, t_l, t_r, t_f)

    def go(h, table, sems, d, i):
        lo, hi, s = table[i]
        lo, hi = cuts[h][lo], cuts[h][hi]
        blocks = ng[h].at[pl.ds(lo, hi - lo), s]
        return rcopy(blocks, blocks, sems[0].at[h, i], sems[1].at[h, i], d)

    xps, xms, zs = (xp_s, xp_r), (xm_s, xm_r), (z_s, z_r)

    def twin(h, i, s):
        blocks = ng[h].at[:, s]
        return rcopy(blocks, blocks, c_s.at[h, i], c_r.at[h, i], d_c)

    def gather_steps(h):
        def send(*what):
            for name, i in what:
                if name == "xp":
                    go(h, to_xp, xps, d_xp, i).start()
                elif name == "xm":
                    go(h, to_xm, xms, d_xm, i).start()
                elif name == "z":
                    go(h, to_z, zs, d_zn, i).start()
                else:
                    twin(h, i, order[i]).start()

        def got(*what):
            for name, i in what:
                if name == "xm":
                    go(h, of_xm, xps, d_xp, i).wait_recv()
                elif name == "xp":
                    go(h, of_xp, xms, d_xm, i).wait_recv()
                else:
                    go(h, of_z, zs, d_zn, i).wait_recv()

        def first():
            p1_wait(h, 0)
            send(("xp", 0), ("xm", 0), ("z", 0))

        def second():
            p1_wait(h, 1)
            send(("xp", 1), ("xm", 1), ("z", 1), ("c", 0))

        def a_sides():
            got(("xm", 0))
            send(("xp", 3), ("z", 2))
            got(("xp", 0))
            send(("xm", 3), ("z", 3))

        def b_sides():
            got(("xm", 1))
            send(("xp", 4), ("c", 1))
            got(("xp", 1))
            send(("xm", 4), ("c", 2))

        def pair():
            got(("z", 0), ("z", 1))
            send(("xp", 2), ("xm", 2), ("c", 3))

        def far_a():
            got(("xm", 3))
            send(("z", 4))
            got(("xp", 3))
            send(("z", 5))

        def pair_sides():
            got(("xm", 2))
            send(("xp", 5))
            got(("xp", 2))
            send(("xm", 5))

        def far_b():
            got(("xm", 4), ("xp", 4))
            send(("c", 4))

        def last_sides():
            got(("z", 2))
            send(("c", 5))
            got(("z", 3))
            send(("c", 6))

        def last_far():
            got(("xm", 5), ("xp", 5), ("z", 4), ("z", 5))
            send(("c", 7))

        return (
            first, second, a_sides, b_sides, pair, far_a, pair_sides, far_b, last_sides, last_far,
        )

    def spread(h):
        for i in range(8):
            twin(h, i, order[i] + 1 - 2 * c).wait_recv()

        def block(i, carry):
            p, t = i // 6, i % 6
            w = tab[2, i]
            v = ng0[jnp.clip(w, 0, FIRST - 1)].reshape(256, 256)
            if h == 1:
                late = ng1[jnp.clip(w - FIRST, 0, KEEP - FIRST - 1)].reshape(256, 256)
                v = jnp.where(w >= FIRST, late, v)
            v = jnp.where(w >= 0, v, 0.0)
            hi, lo = split2(v)
            nhi[p, t] = hi
            nlo[p, t] = lo
            return carry

        lax.fori_loop(12 * h, 12 * h + 12, block, 0)


    rounds = KEEP // QR
    early = KEEP // 3 // QR

    def product(q):
        s, p = tab[0, q], tab[1, q]
        bh = nhi[p].reshape(1536, 256)
        v = jnp.dot(ghi[s], bh, preferred_element_type=F32)
        v += jnp.dot(ghi[s], nlo[p].reshape(1536, 256), preferred_element_type=F32)
        v += jnp.dot(glo[s], bh, preferred_element_type=F32)
        pb[q] = v.reshape(4, 2, 2, 16, 256)

    def m_core(g):
        qs = pl.ds(g * QR, QR)
        return rcopy(pb.at[qs, :, :, 1 - c], rc.at[qs], rs_s.at[0, g], rs_r.at[0, g], d_c)

    def m_a(g):
        qs = pl.ds(g * QR, QR)
        return rcopy(pb.at[qs, yf, 0, c], ra.at[qs], rs_s.at[1, g], rs_r.at[1, g], d_yp)

    def m_b(g):
        qs = pl.ds(g * QR, QR)
        return rcopy(pb.at[qs, yf, 1, c], rb.at[qs], rs_s.at[2, g], rs_r.at[2, g], d_ym)

    def m_p(g):
        qs = pl.ds(g * QR, QR)
        return rcopy(pb.at[qs, yp, :, c], rp.at[qs], rs_s.at[3, g], rs_r.at[3, g], d_yp)

    def m_m(g):
        qs = pl.ds(g * QR, QR)
        return rcopy(pb.at[qs, ym, :, c], rm.at[qs], rs_s.at[4, g], rs_r.at[4, g], d_ym)

    def m_z(g):
        qs = pl.ds(g * QR, QR)
        return rcopy(pb.at[qs, y, 1 - zh, c], rz.at[qs], rs_s.at[5, g], rs_r.at[5, g], d_z2)

    def m_out(g):
        qs = pl.ds(g * QR, QR)
        return rcopy(out.at[qs], outx.at[qs], rs_s.at[6, g], rs_r.at[6, g], d_c)


    def m_down(n):
        return rcopy(
            dw.at[(at[0] + n) % 4], e1.at[n - 1], ar_s.at[n], ar_r.at[n], peer(n, 0, 0)
        )

    def m_plane(n2, n3):
        k = n2 * 4 + n3
        return rcopy(
            dw.at[at[0], (at[1] + n2) % 4, (at[2] + n3) % 4], e2.at[k - 1],
            ar_s.at[3 + k], ar_r.at[3 + k], peer(0, n2, n3),
        )

    def m_plane_up(n2, n3):
        k = n2 * 4 + n3
        part = dout.at[c, at[0], at[1], at[2]]
        return rcopy(part, part, ar_s.at[18 + k], ar_r.at[18 + k], peer(0, n2, n3))

    def m_up(n):
        part = dout.at[c, at[0]]
        return rcopy(part, part, ar_s.at[33 + n], ar_r.at[33 + n], peer(n, 0, 0))

    def m_twin(n):
        part = dout.at[c, (at[0] + 4 - n) % 4]
        return rcopy(part, part, ar_s.at[37 + n], ar_r.at[37 + n], d_c)

    def diagonal():
        for p in range(4):
            for s in range(12):
                w = tab[3, p * 12 + s]
                pid[p, s] = jnp.where(w >= 0, out[jnp.maximum(w, 0)], 0.0)
        m_rows().wait_recv()

        @pl.loop(0, rounds)
        def _(g):
            m_out(g).wait_recv()

        def term(a, b):
            return lax.dot_general(
                a.reshape(192, 256), b.reshape(192, 256), (((0,), (0,)), ((), ())),
                precision=lax.Precision.HIGHEST, preferred_element_type=F32,
            )

        for k in range(2):
            p = 2 * c + k
            for s in range(12):
                w = tab[3, p * 12 + s]
                pt[s] = jnp.where(w >= 0, outx[jnp.maximum(w, 0)], 0.0)
            d = term(nd[p], pid[p]) + term(ndt[k], pt[...])
            dw[2 * k : 2 * k + 2] = d.reshape(2, 4, 4, 8, 256)
        for n in (1, 3, 2):
            m_down(n).start()
        for n in (1, 3, 2):
            m_down(n).wait_recv()
        dw[at[0]] = dw[at[0]] + (e1[0] + e1[1] + e1[2])
        for n in plane:
            m_plane(*n).start()
        for n in plane:
            m_plane(*n).wait_recv()
        total = dw[at[0], at[1], at[2]]
        for k in range(15):
            total = total + e2[k]
        dout[c, at[0], at[1], at[2]] = given[c, at[0], at[1], at[2]] - total
        for n in plane:
            m_plane_up(*n).start()
        for n in plane:
            m_plane_up(*n).wait_recv()
        for n in (1, 3, 2):
            m_up(n).start()
        m_twin(0).start()
        for n in (1, 3, 2):
            m_up(n).wait_recv()
            m_twin(n).start()
        for n in range(4):
            m_twin(n).wait_recv()

    def diagonal_sent():
        m_rows().wait_send()
        for n in (1, 2, 3):
            m_down(n).wait_send()
            m_up(n).wait_send()
        for n in plane:
            m_plane(*n).wait_send()
            m_plane_up(*n).wait_send()
        for n in range(4):
            m_twin(n).wait_send()


    one, two = gather_steps(0), gather_steps(1)
    m_rows().start()
    some_g(0, G_FIRST)
    one[0]()
    some_g(G_FIRST, G_FIRST + 2)
    one[1]()
    left = chunks - G_FIRST - 2
    for n in range(2, 7):
        some_g(G_FIRST + 2 + left * (n - 2) // 5, G_FIRST + 2 + left * (n - 1) // 5)
        one[n]()
    two[0]()
    two[1]()
    for n in range(7, 10):
        one[n]()
    spread(0)

    under = {}
    for n, r in zip(range(2, 10), GATHER_AT):
        under.setdefault(r, []).append(two[n])
    under.setdefault(early, []).append(lambda: spread(1))

    def step(i, carry):
        for r, acts in under.items():

            @pl.when(i == r)
            def _(acts=acts):
                for act in acts:
                    act()

        @pl.when(i < rounds)
        def _():
            @pl.loop(0, QR)
            def _(n):
                product(i * QR + n)

            m_core(i).start()

        @pl.when((i >= LAGS[0]) & (i < rounds + LAGS[0]))
        def _():
            g = i - LAGS[0]
            m_core(g).wait_recv()

            @pl.loop(0, QR)
            def _(n):
                q = g * QR + n
                pb[q, :, :, c] += rc[q]

            m_a(g).start()
            m_b(g).start()

        @pl.when((i >= LAGS[1]) & (i < rounds + LAGS[1]))
        def _():
            g = i - LAGS[1]
            m_a(g).wait_recv()
            m_b(g).wait_recv()

            @pl.loop(0, QR)
            def _(n):
                q = g * QR + n
                pb[q, yp, 0, c] += ra[q]
                pb[q, ym, 1, c] += rb[q]

            m_p(g).start()
            m_m(g).start()

        @pl.when((i >= LAGS[2]) & (i < rounds + LAGS[2]))
        def _():
            g = i - LAGS[2]
            m_p(g).wait_recv()
            m_m(g).wait_recv()

            @pl.loop(0, QR)
            def _(n):
                q = g * QR + n
                pb[q, y, :, c] += rp[q] + rm[q]

            m_z(g).start()

        @pl.when(i >= LAGS[3])
        def _():
            g = i - LAGS[3]
            m_z(g).wait_recv()

            @pl.loop(0, QR)
            def _(n):
                q = g * QR + n
                out[q] = -(pb[q, y, zh, c] + rz[q])

            m_out(g).start()

        return carry

    lax.fori_loop(0, rounds + LAGS[3], step, 0)
    diagonal()

    @pl.when(jnp.logical_not(own_target))
    def _():
        for h in (0, 1):
            p1(h, 0).wait_send()
            p1(h, 1).wait_send()

    for h in (0, 1):
        for i in range(6):
            go(h, to_xp, xps, d_xp, i).wait_send()
            go(h, to_xm, xms, d_xm, i).wait_send()
            go(h, to_z, zs, d_zn, i).wait_send()
        for i in range(8):
            twin(h, i, order[i]).wait_send()

    @pl.loop(0, rounds)
    def _(g):
        m_core(g).wait_send()
        m_a(g).wait_send()
        m_b(g).wait_send()
        m_p(g).wait_send()
        m_m(g).wait_send()
        m_z(g).wait_send()
        m_out(g).wait_send()

    diagonal_sent()


VM = pl.BlockSpec(memory_space=pltpu.VMEM)
SM = pl.BlockSpec(memory_space=pltpu.SMEM)
ANY = pl.BlockSpec(memory_space=pl.ANY)
DMA = pltpu.SemaphoreType.DMA
G_FIRST = 10
GATHER_AT = (1, 1, 2, 2, 3, 3, 4, 4)


def on_device(
    inverse_matrix, factor_blocks, factor_inverse, diag_given, block_lists, list_mask, slot_of_block
):
    k = lax.axis_index("prow")
    j = lax.axis_index("pcol")
    valid = valid_slots(block_lists, list_mask, slot_of_block)
    pos_row, idx = packed_order(valid, k)
    pos_col, _ = packed_order(valid, j // 2)
    s_q = idx % 12
    p_q = idx // 12
    col = lax.dynamic_slice_in_dim(pos_col.reshape(4, 12), (j % 2) * 6, 6, 1).reshape(24)
    tab = jnp.stack(
        [jnp.pad(s_q, (0, 12)), jnp.pad(p_q, (0, 12)), jnp.pad(col, (0, 24)), pos_row]
    )

    nc, nd = pl.pallas_call(
        prep_kernel,
        out_shape=(
            jax.ShapeDtypeStruct((KEEP, 16, 256), F32),
            jax.ShapeDtypeStruct((4, 12, 16, 256), F32),
        ),
        in_specs=[SM, VM, VM],
        out_specs=(VM, VM),
        name="normalize",
    )(tab, factor_blocks, factor_inverse)

    rounds = KEEP // QR
    panel_inverse, diag = pl.pallas_call(
        main_kernel,
        out_shape=(
            jax.ShapeDtypeStruct((4, 12, 16, 256), F32),
            jax.ShapeDtypeStruct((2, 4, 4, 4, 8, 256), F32),
        ),
        in_specs=[SM, ANY, VM, VM, VM],
        out_specs=(VM, VM),
        scratch_shapes=[
            pltpu.VMEM((KEEP, 16, 256), F32),
            pltpu.VMEM((12, 256, 1536), BF16),
            pltpu.VMEM((12, 256, 1536), BF16),
            pltpu.VMEM((STAGES, ROWS, 1536), F32),
            pltpu.VMEM((FIRST, 16, 16, 256), F32),
            pltpu.VMEM((KEEP - FIRST, 16, 16, 256), F32),
            pltpu.VMEM((4, 6, 256, 256), BF16),
            pltpu.VMEM((4, 6, 256, 256), BF16),
            pltpu.VMEM((KEEP, 4, 2, 2, 16, 256), F32),
            pltpu.VMEM((KEEP, 4, 2, 16, 256), F32),
            pltpu.VMEM((KEEP, 16, 256), F32),
            pltpu.VMEM((KEEP, 16, 256), F32),
            pltpu.VMEM((KEEP, 2, 16, 256), F32),
            pltpu.VMEM((KEEP, 2, 16, 256), F32),
            pltpu.VMEM((KEEP, 16, 256), F32),
            pltpu.VMEM((KEEP, 16, 256), F32),
            pltpu.VMEM((2, 12, 16, 256), F32),
            pltpu.VMEM((12, 16, 256), F32),
            pltpu.VMEM((4, 4, 4, 8, 256), F32),
            pltpu.VMEM((3, 4, 4, 8, 256), F32),
            pltpu.VMEM((15, 8, 256), F32),
            DMA((STAGES,)),
            DMA((2, 2)),
            DMA((2, 2)),
            DMA((2, 6)),
            DMA((2, 6)),
            DMA((2, 6)),
            DMA((2, 6)),
            DMA((2, 6)),
            DMA((2, 6)),
            DMA((2, 8)),
            DMA((2, 8)),
            DMA((7, rounds)),
            DMA((7, rounds)),
            DMA((41,)),
            DMA((41,)),
        ],
        compiler_params=pltpu.CompilerParams(
            collective_id=0, has_side_effects=True, vmem_limit_bytes=67043328
        ),
        name="window",
    )(tab, inverse_matrix, nc, nd, diag_given.reshape(2, 4, 4, 4, 8, 256))
    return (panel_inverse, diag.reshape(4, 256, 256))


def solution(mesh):
    return jax.shard_map(
        on_device,
        mesh=mesh,
        in_specs=(P("prow", "pcol"), P(None, "prow", "pcol", None), P(), P(), P(), P(), P()),
        out_specs=(P(None, "prow", "pcol", None), P()),
        check_vma=False,
    )
```

```python
import functools

import jax
import jax.numpy as jnp
from jax import lax
from jax.experimental import pallas as pl
from jax.experimental.pallas import tpu as pltpu
from jax.sharding import PartitionSpec as P

MESH = pl.DeviceIdType.MESH
F32 = jnp.float32
BF16 = jnp.bfloat16
KEEP = 36
FIRST = 24
QR = 3
STAGES = 4
ROWS = 128
LAGS = (1, 3, 5, 7)


def coords():
    k = lax.axis_index("prow")
    j = lax.axis_index("pcol")
    return k // 2, j // 4, (j // 2) % 2, k % 2, j % 2


def dev(x, y, zh, zl, c):
    return (x * 2 + zl, (y * 2 + zh) * 2 + c)


def split2(v):
    hi = v.astype(BF16)
    lo = (v - hi.astype(F32)).astype(BF16)
    return hi, lo


def valid_slots(block_lists, list_mask, slot_of_block):
    window_blocks = block_lists.shape[1]
    block_ids = jnp.arange(window_blocks, dtype=jnp.int32)
    chosen = (block_lists[:, :, None] == block_ids[None, None, :]).astype(jnp.int32)
    slot_ids = jnp.sum(chosen * slot_of_block[None, None, :], axis=2)
    matches = (slot_ids[:, :, None] == block_ids[None, None, :]).astype(jnp.int32) * list_mask[
        :, :, None
    ]
    return jnp.sum(matches, axis=1)


def packed_order(valid, group):
    v = lax.dynamic_slice_in_dim(valid, group * 12, 12, 1).reshape(48)
    i = jnp.arange(48, dtype=jnp.int32)
    pos = jnp.sum(v[None, :] * (i[None, :] < i[:, None]).astype(jnp.int32), axis=1)
    q = jnp.arange(KEEP, dtype=jnp.int32)
    hit = (pos[None, :] == q[:, None]).astype(jnp.int32) * v[None, :]
    idx = jnp.sum(hit * i[None, :], axis=1)
    return jnp.where(v > 0, pos, -1), idx


def main_kernel(
    tab, g_hbm, f_hbm, inv_hbm, given, pid, dout,
    nd, inv, nc, gv, out, ghi, glo, stage, ng0, ng1, nhi, nlo, pb, rc, ra, rb, rp, rm, rz, outx, ndt, pt, dw, dsum, e1, e2,
    in_sem, g_sem, p1_s, p1_r, xp_s, xp_r, xm_s, xm_r, z_s, z_r, c_s, c_r, rs_s, rs_r, ar_s, ar_r,
):
    x, y, zh, zl, c = coords()
    z = 2 * zh + zl
    xp, xm, xf = (x + 1) % 4, (x + 3) % 4, (x + 2) % 4
    yp, ym, yf = (y + 1) % 4, (y + 3) % 4, (y + 2) % 4
    zn = 1 - zl
    d_xp, d_xm = dev(xp, y, zh, zl, c), dev(xm, y, zh, zl, c)
    d_zn, d_c = dev(x, y, zh, zn, c), dev(x, y, zh, zl, 1 - c)
    d_yp, d_ym = dev(x, yp, zh, zl, c), dev(x, ym, zh, zl, c)
    d_z2 = dev(x, y, 1 - zh, zl, c)
    d_to = dev((y + 2 * (x % 2)) % 4, x, zl, zh, c)
    d_from = dev(y, (x + 2 * (y % 2)) % 4, zl, zh, c)
    own_target = ((x == y) & (x % 2 == 0)) & (zl == zh)

    at = (jnp.where(c == 0, x, y), jnp.where(c == 0, y, x), z)

    def peer(n1, n2, n3):
        a, b, e = (at[0] + n1) % 4, (at[1] + n2) % 4, (at[2] + n3) % 4
        return dev(jnp.where(c == 0, a, b), jnp.where(c == 0, b, a), e // 2, e % 2, c)

    plane = [(n2, n3) for n2 in range(4) for n3 in range(4) if (n2, n3) != (0, 0)]

    barrier = pltpu.get_barrier_semaphore()
    for d in [d_c] + [peer(n, 0, 0) for n in (1, 2, 3)] + [peer(0, *n) for n in plane]:
        pl.semaphore_signal(barrier, inc=1, device_id=d, device_id_type=MESH)

    @pl.when(jnp.logical_not(own_target))
    def _():
        for d in (d_to, d_from):
            pl.semaphore_signal(barrier, inc=1, device_id=d, device_id_type=MESH)

    ins = (
        pltpu.make_async_copy(f_hbm, nd, in_sem.at[0]),
        pltpu.make_async_copy(inv_hbm, inv, in_sem.at[1]),
        pltpu.make_async_copy(given.at[c, at[0], at[1], at[2]], gv, in_sem.at[2]),
    )
    for cp in ins:
        cp.start()

    chunks = 3072 // ROWS

    def g_copy(i):
        slot = i % STAGES
        return pltpu.make_async_copy(
            g_hbm.at[pl.ds(i * ROWS, ROWS), :], stage.at[slot], g_sem.at[slot]
        )

    for n in range(STAGES - 1):
        g_copy(n).start()

    for cp in ins:
        cp.wait()
    for p in range(4):
        nd[p] = jnp.dot(
            nd[p].reshape(192, 256),
            inv[p],
            precision=lax.Precision.HIGHEST,
            preferred_element_type=F32,
        ).reshape(12, 16, 256)

    @pl.loop(0, KEEP)
    def _(q):
        nc[q] = nd[tab[1, q], tab[0, q]]

    @pl.when(jnp.logical_not(own_target))
    def _():
        pl.semaphore_wait(barrier, 21)

    @pl.when(own_target)
    def _():
        pl.semaphore_wait(barrier, 19)

    def share(xx, zz):
        return 2 * (2 * ((xx + 2 * (y % 2)) % 4) + zz) + c

    r_me = (y * 2 + zh) * 2 + c
    s_o, s_l, s_r, s_f = (share(v, zl) for v in (x, xm, xp, xf))
    t_o, t_l, t_r, t_f = (share(v, zn) for v in (x, xm, xp, xf))
    cuts = ((0, 5, 10, 17, 24), (0, 3, 6, 9, 12))
    ng = (ng0, ng1)
    base = (0, FIRST)

    def rcopy(src, dst, ss, rs, d):
        return pltpu.make_async_remote_copy(
            src_ref=src, dst_ref=dst, send_sem=ss, recv_sem=rs, device_id=d, device_id_type=MESH
        )


    spans = tuple(((v[0], v[2]), (v[2], v[4])) for v in cuts)

    def p1(h, i):
        lo, hi = spans[h][i]
        return rcopy(
            nc.at[pl.ds(base[h] + lo, hi - lo)], ng[h].at[pl.ds(lo, hi - lo), r_me],
            p1_s.at[h, i], p1_r.at[h, i], d_to,
        )

    def p1_local(h, i):
        lo, hi = spans[h][i]
        return pltpu.make_async_copy(
            nc.at[pl.ds(base[h] + lo, hi - lo)], ng[h].at[pl.ds(lo, hi - lo), s_o], p1_r.at[h, i]
        )

    def m_rows():
        return rcopy(nd.at[pl.ds(2 * (1 - c), 2)], ndt, ar_s.at[0, 0], ar_r.at[0, 0], d_c)

    @pl.when(jnp.logical_not(own_target))
    def _():
        for h in (0, 1):
            for i in (1, 0):
                p1(h, i).start()

    @pl.when(own_target)
    def _():
        for h in (0, 1):
            for i in (1, 0):
                p1_local(h, i).start()

    def p1_wait(h, i):
        @pl.when(jnp.logical_not(own_target))
        def _():
            p1(h, i).wait_recv()

        @pl.when(own_target)
        def _():
            p1_local(h, i).wait()


    def load_g(i, carry):
        g_copy(i).wait()

        @pl.when(i < chunks - STAGES + 1)
        def _():
            g_copy(i + STAGES - 1).start()

        per = 256 // ROWS
        b, r0 = i // per, (i % per) * ROWS
        for r in range(0, ROWS, 64):
            hi, lo = split2(stage[i % STAGES, r : r + 64, :])
            at = pl.ds(pl.multiple_of(r0 + r, 64), 64)
            ghi[b, at, :] = hi
            glo[b, at, :] = lo
        return carry

    def some_g(lo, hi):
        lax.fori_loop(lo, hi, load_g, 0)


    to_xp = ((0, 2, s_o), (2, 4, s_o), (2, 4, t_o), (0, 1, s_l), (2, 3, s_l), (2, 3, t_l))
    to_xm = ((0, 2, s_o), (2, 4, s_o), (2, 4, t_o), (1, 2, s_r), (3, 4, s_r), (3, 4, t_r))
    to_z = ((0, 2, s_o), (2, 4, s_o), (0, 2, s_l), (0, 2, s_r), (0, 1, s_f), (1, 2, s_f))
    of_xm = ((0, 2, s_l), (2, 4, s_l), (2, 4, t_l), (0, 1, s_f), (2, 3, s_f), (2, 3, t_f))
    of_xp = ((0, 2, s_r), (2, 4, s_r), (2, 4, t_r), (1, 2, s_f), (3, 4, s_f), (3, 4, t_f))
    of_z = ((0, 2, t_o), (2, 4, t_o), (0, 2, t_l), (0, 2, t_r), (0, 1, t_f), (1, 2, t_f))
    order = (s_o, s_l, s_r, t_o, s_f, t_l, t_r, t_f)

    def go(h, table, sems, d, i):
        lo, hi, s = table[i]
        lo, hi = cuts[h][lo], cuts[h][hi]
        blocks = ng[h].at[pl.ds(lo, hi - lo), s]
        return rcopy(blocks, blocks, sems[0].at[h, i], sems[1].at[h, i], d)

    xps, xms, zs = (xp_s, xp_r), (xm_s, xm_r), (z_s, z_r)

    def twin(h, i, s):
        blocks = ng[h].at[:, s]
        return rcopy(blocks, blocks, c_s.at[h, i], c_r.at[h, i], d_c)

    def gather_steps(h):
        def send(*what):
            for name, i in what:
                if name == "xp":
                    go(h, to_xp, xps, d_xp, i).start()
                elif name == "xm":
                    go(h, to_xm, xms, d_xm, i).start()
                elif name == "z":
                    go(h, to_z, zs, d_zn, i).start()
                else:
                    twin(h, i, order[i]).start()

        def got(*what):
            for name, i in what:
                if name == "xm":
                    go(h, of_xm, xps, d_xp, i).wait_recv()
                elif name == "xp":
                    go(h, of_xp, xms, d_xm, i).wait_recv()
                else:
                    go(h, of_z, zs, d_zn, i).wait_recv()

        def first():
            p1_wait(h, 1)
            send(("xp", 1), ("xm", 1), ("z", 1))

        def second():
            p1_wait(h, 0)
            send(("xp", 0), ("xm", 0), ("z", 0), ("c", 0))

        def b_sides():
            got(("xm", 1))
            send(("xp", 4))
            got(("xp", 1))
            send(("xm", 4))

        def b_pair():
            got(("z", 1))
            send(("xp", 2), ("xm", 2))

        def a_sides():
            got(("xm", 0))
            send(("xp", 3), ("z", 2), ("c", 1))
            got(("xp", 0))
            send(("xm", 3), ("z", 3), ("c", 2))

        def a_pair():
            got(("z", 0))
            send(("c", 3))

        def pair_sides():
            got(("xm", 2))
            send(("xp", 5))
            got(("xp", 2))
            send(("xm", 5))

        def far():
            got(("xm", 4), ("xp", 4), ("xm", 3))
            send(("z", 4))
            got(("xp", 3))
            send(("z", 5), ("c", 4))

        def last_sides():
            got(("z", 2))
            send(("c", 5))
            got(("z", 3))
            send(("c", 6))

        def last_far():
            got(("xm", 5), ("xp", 5), ("z", 4), ("z", 5))
            send(("c", 7))

        return (
            first, second, b_sides, b_pair, a_sides, a_pair, pair_sides, far, last_sides, last_far,
        )

    def spread(h):
        for i in range(8):
            twin(h, i, order[i] + 1 - 2 * c).wait_recv()

        def block(i, carry):
            p, t = i // 6, i % 6
            w = tab[2, i]
            v = ng0[jnp.clip(w, 0, FIRST - 1)].reshape(256, 256)
            if h == 1:
                late = ng1[jnp.clip(w - FIRST, 0, KEEP - FIRST - 1)].reshape(256, 256)
                v = jnp.where(w >= FIRST, late, v)
            v = jnp.where(w >= 0, v, 0.0)
            hi, lo = split2(v)
            nhi[p, t] = hi
            nlo[p, t] = lo
            return carry

        lax.fori_loop(12 * h, 12 * h + 12, block, 0)


    rounds = KEEP // QR
    early = KEEP // 3 // QR

    def product(q):
        s, p = tab[0, q], tab[1, q]
        bh = nhi[p].reshape(1536, 256)
        v = jnp.dot(ghi[s], bh, preferred_element_type=F32)
        v += jnp.dot(ghi[s], nlo[p].reshape(1536, 256), preferred_element_type=F32)
        v += jnp.dot(glo[s], bh, preferred_element_type=F32)
        pb[q] = v.reshape(4, 2, 2, 16, 256)

    def m_core(g):
        qs = pl.ds(g * QR, QR)
        return rcopy(pb.at[qs, :, :, 1 - c], rc.at[qs], rs_s.at[0, g], rs_r.at[0, g], d_c)

    def m_a(g):
        qs = pl.ds(g * QR, QR)
        return rcopy(pb.at[qs, yf, 0, c], ra.at[qs], rs_s.at[1, g], rs_r.at[1, g], d_yp)

    def m_b(g):
        qs = pl.ds(g * QR, QR)
        return rcopy(pb.at[qs, yf, 1, c], rb.at[qs], rs_s.at[2, g], rs_r.at[2, g], d_ym)

    def m_p(g):
        qs = pl.ds(g * QR, QR)
        return rcopy(pb.at[qs, yp, :, c], rp.at[qs], rs_s.at[3, g], rs_r.at[3, g], d_yp)

    def m_m(g):
        qs = pl.ds(g * QR, QR)
        return rcopy(pb.at[qs, ym, :, c], rm.at[qs], rs_s.at[4, g], rs_r.at[4, g], d_ym)

    def m_z(g):
        qs = pl.ds(g * QR, QR)
        return rcopy(pb.at[qs, y, 1 - zh, c], rz.at[qs], rs_s.at[5, g], rs_r.at[5, g], d_z2)

    def m_out(g):
        qs = pl.ds(g * QR, QR)
        return rcopy(out.at[qs], outx.at[qs], rs_s.at[6, g], rs_r.at[6, g], d_c)


    def m_down(n, w):
        return rcopy(
            dw.at[w, (at[0] + n) % 4], e1.at[w, n - 1], ar_s.at[w, n], ar_r.at[w, n], peer(n, 0, 0)
        )

    def m_plane(n2, n3, w):
        k = n2 * 4 + n3
        return rcopy(
            dw.at[w, at[0], (at[1] + n2) % 4, (at[2] + n3) % 4], e2.at[w, k - 1],
            ar_s.at[w, 3 + k], ar_r.at[w, 3 + k], peer(0, n2, n3),
        )

    def m_plane_up(n2, n3, w):
        k = n2 * 4 + n3
        part = dsum.at[w, c, at[0], at[1], at[2]]
        return rcopy(part, part, ar_s.at[w, 18 + k], ar_r.at[w, 18 + k], peer(0, n2, n3))

    def m_up(n, w):
        part = dsum.at[w, c, at[0]]
        return rcopy(part, part, ar_s.at[w, 33 + n], ar_r.at[w, 33 + n], peer(n, 0, 0))

    def m_twin(n, w):
        part = dsum.at[w, c, (at[0] + 4 - n) % 4]
        return rcopy(part, part, ar_s.at[w, 37 + n], ar_r.at[w, 37 + n], d_c)

    def diagonal():
        for p in range(4):
            for s in range(12):
                w = tab[3, p * 12 + s]
                pid[p, s] = jnp.where(w >= 0, out[jnp.maximum(w, 0)], 0.0)
        m_rows().wait_recv()

        @pl.loop(0, rounds)
        def _(g):
            m_out(g).wait_recv()

        def term(a, b):
            return lax.dot_general(
                a.reshape(192, 256), b.reshape(192, 256), (((0,), (0,)), ((), ())),
                precision=lax.Precision.HIGHEST, preferred_element_type=F32,
            )

        for k in range(2):
            p = 2 * c + k
            for s in range(12):
                w = tab[3, p * 12 + s]
                pt[s] = jnp.where(w >= 0, outx[jnp.maximum(w, 0)], 0.0)
            d = term(nd[p], pid[p]) + term(ndt[k], pt[...])
            for w in (0, 1):
                dw[w, 2 * k : 2 * k + 2] = d[:, 128 * w : 128 * w + 128].reshape(2, 4, 4, 8, 128)
        both = (0, 1)
        for w in both:
            for n in (1, 3, 2):
                m_down(n, w).start()
        for w in both:
            for n in (1, 3, 2):
                m_down(n, w).wait_recv()
            dw[w, at[0]] = dw[w, at[0]] + (e1[w, 0] + e1[w, 1] + e1[w, 2])
            for n in plane:
                m_plane(*n, w).start()
        for w in both:
            for n in plane:
                m_plane(*n, w).wait_recv()
            total = dw[w, at[0], at[1], at[2]]
            for k in range(15):
                total = total + e2[w, k]
            dsum[w, c, at[0], at[1], at[2]] = gv[:, 128 * w : 128 * w + 128] - total
            for n in plane:
                m_plane_up(*n, w).start()
        for w in both:
            for n in plane:
                m_plane_up(*n, w).wait_recv()
            for n in (1, 3, 2):
                m_up(n, w).start()
            m_twin(0, w).start()
        for w in both:
            for n in (1, 3, 2):
                m_up(n, w).wait_recv()
                m_twin(n, w).start()
        for w in both:
            for n in range(4):
                m_twin(n, w).wait_recv()
            dout[:, :, :, :, :, 128 * w : 128 * w + 128] = dsum[w]

    def diagonal_sent():
        m_rows().wait_send()
        for w in (0, 1):
            for n in (1, 2, 3):
                m_down(n, w).wait_send()
                m_up(n, w).wait_send()
            for n in plane:
                m_plane(*n, w).wait_send()
                m_plane_up(*n, w).wait_send()
            for n in range(4):
                m_twin(n, w).wait_send()


    one, two = gather_steps(0), gather_steps(1)
    m_rows().start()
    some_g(0, G_FIRST)
    one[0]()
    some_g(G_FIRST, G_FIRST + 2)
    one[1]()
    left = chunks - G_FIRST - 2
    for n in range(2, 7):
        some_g(G_FIRST + 2 + left * (n - 2) // 5, G_FIRST + 2 + left * (n - 1) // 5)
        one[n]()
    two[0]()
    two[1]()
    for n in range(7, 10):
        one[n]()
    spread(0)

    under = {}
    for n, r in zip(range(2, 10), GATHER_AT):
        under.setdefault(r, []).append(two[n])
    under.setdefault(early, []).append(lambda: spread(1))

    def step(i, carry):
        for r, acts in under.items():

            @pl.when(i == r)
            def _(acts=acts):
                for act in acts:
                    act()

        @pl.when(i < rounds)
        def _():
            @pl.loop(0, QR)
            def _(n):
                product(i * QR + n)

            m_core(i).start()

        @pl.when((i >= LAGS[0]) & (i < rounds + LAGS[0]))
        def _():
            g = i - LAGS[0]
            m_core(g).wait_recv()

            @pl.loop(0, QR)
            def _(n):
                q = g * QR + n
                pb[q, :, :, c] += rc[q]

            m_a(g).start()
            m_b(g).start()

        @pl.when((i >= LAGS[1]) & (i < rounds + LAGS[1]))
        def _():
            g = i - LAGS[1]
            m_a(g).wait_recv()
            m_b(g).wait_recv()

            @pl.loop(0, QR)
            def _(n):
                q = g * QR + n
                pb[q, yp, 0, c] += ra[q]
                pb[q, ym, 1, c] += rb[q]

            m_p(g).start()
            m_m(g).start()

        @pl.when((i >= LAGS[2]) & (i < rounds + LAGS[2]))
        def _():
            g = i - LAGS[2]
            m_p(g).wait_recv()
            m_m(g).wait_recv()

            @pl.loop(0, QR)
            def _(n):
                q = g * QR + n
                pb[q, y, :, c] += rp[q] + rm[q]

            m_z(g).start()

        @pl.when(i >= LAGS[3])
        def _():
            g = i - LAGS[3]
            m_z(g).wait_recv()

            @pl.loop(0, QR)
            def _(n):
                q = g * QR + n
                out[q] = -(pb[q, y, zh, c] + rz[q])

            m_out(g).start()

        return carry

    lax.fori_loop(0, rounds + LAGS[3], step, 0)
    diagonal()

    @pl.when(jnp.logical_not(own_target))
    def _():
        for h in (0, 1):
            p1(h, 0).wait_send()
            p1(h, 1).wait_send()

    for h in (0, 1):
        for i in range(6):
            go(h, to_xp, xps, d_xp, i).wait_send()
            go(h, to_xm, xms, d_xm, i).wait_send()
            go(h, to_z, zs, d_zn, i).wait_send()
        for i in range(8):
            twin(h, i, order[i]).wait_send()

    @pl.loop(0, rounds)
    def _(g):
        m_core(g).wait_send()
        m_a(g).wait_send()
        m_b(g).wait_send()
        m_p(g).wait_send()
        m_m(g).wait_send()
        m_z(g).wait_send()
        m_out(g).wait_send()

    diagonal_sent()


def results_kernel(a, b, a_out, b_out):
    a_out[...] = a[...]
    b_out[...] = b[...]


VM = pl.BlockSpec(memory_space=pltpu.VMEM)
SM = pl.BlockSpec(memory_space=pltpu.SMEM)
ANY = pl.BlockSpec(memory_space=pl.ANY)
DMA = pltpu.SemaphoreType.DMA
G_FIRST = 10
GATHER_AT = (1, 1, 2, 2, 3, 3, 4, 4)


def on_device(
    inverse_matrix, factor_blocks, factor_inverse, diag_given, block_lists, list_mask, slot_of_block
):
    k = lax.axis_index("prow")
    j = lax.axis_index("pcol")
    valid = valid_slots(block_lists, list_mask, slot_of_block)
    pos_row, idx = packed_order(valid, k)
    pos_col, _ = packed_order(valid, j // 2)
    s_q = idx % 12
    p_q = idx // 12
    col = lax.dynamic_slice_in_dim(pos_col.reshape(4, 12), (j % 2) * 6, 6, 1).reshape(24)
    tab = jnp.stack(
        [jnp.pad(s_q, (0, 12)), jnp.pad(p_q, (0, 12)), jnp.pad(col, (0, 24)), pos_row]
    )

    rounds = KEEP // QR
    results = pl.pallas_call(
        main_kernel,
        out_shape=(
            jax.ShapeDtypeStruct((4, 12, 16, 256), F32),
            jax.ShapeDtypeStruct((2, 4, 4, 4, 8, 256), F32),
        ),
        in_specs=[SM, ANY, ANY, ANY, ANY],
        out_specs=(VM, VM),
        scratch_shapes=[
            pltpu.VMEM((4, 12, 16, 256), F32),
            pltpu.VMEM((4, 256, 256), F32),
            pltpu.VMEM((KEEP, 16, 256), F32),
            pltpu.VMEM((8, 256), F32),
            pltpu.VMEM((KEEP, 16, 256), F32),
            pltpu.VMEM((12, 256, 1536), BF16),
            pltpu.VMEM((12, 256, 1536), BF16),
            pltpu.VMEM((STAGES, ROWS, 1536), F32),
            pltpu.VMEM((FIRST, 16, 16, 256), F32),
            pltpu.VMEM((KEEP - FIRST, 16, 16, 256), F32),
            pltpu.VMEM((4, 6, 256, 256), BF16),
            pltpu.VMEM((4, 6, 256, 256), BF16),
            pltpu.VMEM((KEEP, 4, 2, 2, 16, 256), F32),
            pltpu.VMEM((KEEP, 4, 2, 16, 256), F32),
            pltpu.VMEM((KEEP, 16, 256), F32),
            pltpu.VMEM((KEEP, 16, 256), F32),
            pltpu.VMEM((KEEP, 2, 16, 256), F32),
            pltpu.VMEM((KEEP, 2, 16, 256), F32),
            pltpu.VMEM((KEEP, 16, 256), F32),
            pltpu.VMEM((KEEP, 16, 256), F32),
            pltpu.VMEM((2, 12, 16, 256), F32),
            pltpu.VMEM((12, 16, 256), F32),
            pltpu.VMEM((2, 4, 4, 4, 8, 128), F32),
            pltpu.VMEM((2, 2, 4, 4, 4, 8, 128), F32),
            pltpu.VMEM((2, 3, 4, 4, 8, 128), F32),
            pltpu.VMEM((2, 15, 8, 128), F32),
            DMA((3,)),
            DMA((STAGES,)),
            DMA((2, 2)),
            DMA((2, 2)),
            DMA((2, 6)),
            DMA((2, 6)),
            DMA((2, 6)),
            DMA((2, 6)),
            DMA((2, 6)),
            DMA((2, 6)),
            DMA((2, 8)),
            DMA((2, 8)),
            DMA((7, rounds)),
            DMA((7, rounds)),
            DMA((2, 41)),
            DMA((2, 41)),
        ],
        compiler_params=pltpu.CompilerParams(
            collective_id=0, has_side_effects=True, vmem_limit_bytes=67043328
        ),
        name="window",
    )(tab, inverse_matrix, factor_blocks, factor_inverse, diag_given.reshape(2, 4, 4, 4, 8, 256))
    panel_inverse, diag = pl.pallas_call(
        results_kernel,
        out_shape=tuple(jax.ShapeDtypeStruct(v.shape, F32) for v in results),
        in_specs=[VM, VM],
        out_specs=(VM, VM),
        name="results",
    )(*results)
    return (panel_inverse, diag.reshape(4, 256, 256))


def solution(mesh):
    return jax.shard_map(
        on_device,
        mesh=mesh,
        in_specs=(P("prow", "pcol"), P(None, "prow", "pcol", None), P(), P(), P(), P(), P()),
        out_specs=(P(None, "prow", "pcol", None), P()),
        check_vma=False,
    )
```

```python
import functools

import jax
import jax.numpy as jnp
from jax import lax
from jax.experimental import pallas as pl
from jax.experimental.pallas import tpu as pltpu
from jax.sharding import PartitionSpec as P

MESH = pl.DeviceIdType.MESH
F32 = jnp.float32
BF16 = jnp.bfloat16
KEEP = 36
FIRST = 24
QR = 2
STAGES = 3
ROWS = 128
LAGS = (1, 3, 5, 7)


def coords():
    k = lax.axis_index("prow")
    j = lax.axis_index("pcol")
    return k // 2, j // 4, (j // 2) % 2, k % 2, j % 2


def dev(x, y, zh, zl, c):
    return (x * 2 + zl, (y * 2 + zh) * 2 + c)


def split2(v):
    hi = v.astype(BF16)
    lo = (v - hi.astype(F32)).astype(BF16)
    return hi, lo


def valid_slots(block_lists, list_mask, slot_of_block):
    window_blocks = block_lists.shape[1]
    block_ids = jnp.arange(window_blocks, dtype=jnp.int32)
    chosen = (block_lists[:, :, None] == block_ids[None, None, :]).astype(jnp.int32)
    slot_ids = jnp.sum(chosen * slot_of_block[None, None, :], axis=2)
    matches = (slot_ids[:, :, None] == block_ids[None, None, :]).astype(jnp.int32) * list_mask[
        :, :, None
    ]
    return jnp.sum(matches, axis=1)


def packed_order(valid, group):
    v = lax.dynamic_slice_in_dim(valid, group * 12, 12, 1).reshape(48)
    i = jnp.arange(48, dtype=jnp.int32)
    pos = jnp.sum(v[None, :] * (i[None, :] < i[:, None]).astype(jnp.int32), axis=1)
    q = jnp.arange(KEEP, dtype=jnp.int32)
    hit = (pos[None, :] == q[:, None]).astype(jnp.int32) * v[None, :]
    idx = jnp.sum(hit * i[None, :], axis=1)
    return jnp.where(v > 0, pos, -1), idx


def main_kernel(
    tab, g_hbm, f_hbm, inv_hbm, given, pid, dout,
    nd, inv, nc, gv, out, ghi, glo, stage, ng0, ng1, nhi, nlo, pb, rc, ra, rb, rp, rm, rz, outx0, outx1, ndt, pt, dw, dsum, e1, e2,
    in_sem, g_sem, p1_s, p1_r, xp_s, xp_r, xm_s, xm_r, z_s, z_r, c_s, c_r, rs_s, rs_r, ar_s, ar_r,
):
    x, y, zh, zl, c = coords()
    z = 2 * zh + zl
    xp, xm, xf = (x + 1) % 4, (x + 3) % 4, (x + 2) % 4
    yp, ym, yf = (y + 1) % 4, (y + 3) % 4, (y + 2) % 4
    zn = 1 - zl
    d_xp, d_xm = dev(xp, y, zh, zl, c), dev(xm, y, zh, zl, c)
    d_zn, d_c = dev(x, y, zh, zn, c), dev(x, y, zh, zl, 1 - c)
    d_yp, d_ym = dev(x, yp, zh, zl, c), dev(x, ym, zh, zl, c)
    d_z2 = dev(x, y, 1 - zh, zl, c)
    d_to = dev((y + 2 * (x % 2)) % 4, x, zl, zh, c)
    d_from = dev(y, (x + 2 * (y % 2)) % 4, zl, zh, c)
    own_target = ((x == y) & (x % 2 == 0)) & (zl == zh)

    at = (jnp.where(c == 0, x, y), jnp.where(c == 0, y, x), z)

    def peer(n1, n2, n3):
        a, b, e = (at[0] + n1) % 4, (at[1] + n2) % 4, (at[2] + n3) % 4
        return dev(jnp.where(c == 0, a, b), jnp.where(c == 0, b, a), e // 2, e % 2, c)

    plane = [(n2, n3) for n2 in range(4) for n3 in range(4) if (n2, n3) != (0, 0)]

    barrier = pltpu.get_barrier_semaphore()
    for d in [d_c] + [peer(n, 0, 0) for n in (1, 2, 3)] + [peer(0, *n) for n in plane]:
        pl.semaphore_signal(barrier, inc=1, device_id=d, device_id_type=MESH)

    @pl.when(jnp.logical_not(own_target))
    def _():
        for d in (d_to, d_from):
            pl.semaphore_signal(barrier, inc=1, device_id=d, device_id_type=MESH)

    ins = (
        pltpu.make_async_copy(f_hbm, nd, in_sem.at[0]),
        pltpu.make_async_copy(inv_hbm, inv, in_sem.at[1]),
        pltpu.make_async_copy(given.at[c, at[0] % 2, at[1], at[2]], gv.at[0], in_sem.at[2]),
        pltpu.make_async_copy(given.at[2 + c, at[0] % 2, at[1], at[2]], gv.at[1], in_sem.at[3]),
    )
    for cp in ins:
        cp.start()

    chunks = 3072 // ROWS

    def g_copy(i):
        slot = i % STAGES
        return pltpu.make_async_copy(
            g_hbm.at[pl.ds(i * ROWS, ROWS), :], stage.at[slot], g_sem.at[slot]
        )

    for n in range(STAGES - 1):
        g_copy(n).start()

    for cp in ins:
        cp.wait()
    for p in range(4):
        nd[p] = jnp.dot(
            nd[p].reshape(192, 256),
            inv[p],
            precision=lax.Precision.HIGHEST,
            preferred_element_type=F32,
        ).reshape(12, 16, 256)

    @pl.loop(0, KEEP)
    def _(q):
        nc[q] = nd[tab[1, q], tab[0, q]]

    @pl.when(jnp.logical_not(own_target))
    def _():
        pl.semaphore_wait(barrier, 21)

    @pl.when(own_target)
    def _():
        pl.semaphore_wait(barrier, 19)

    def share(xx, zz):
        return 2 * (2 * ((xx + 2 * (y % 2)) % 4) + zz) + c

    r_me = (y * 2 + zh) * 2 + c
    s_o, s_l, s_r, s_f = (share(v, zl) for v in (x, xm, xp, xf))
    t_o, t_l, t_r, t_f = (share(v, zn) for v in (x, xm, xp, xf))
    cuts = ((0, 5, 10, 17, 24), (0, 3, 6, 9, 12))
    ng = (ng0, ng1)
    base = (0, FIRST)

    def rcopy(src, dst, ss, rs, d):
        return pltpu.make_async_remote_copy(
            src_ref=src, dst_ref=dst, send_sem=ss, recv_sem=rs, device_id=d, device_id_type=MESH
        )


    spans = tuple(((v[0], v[2]), (v[2], v[4])) for v in cuts)

    def p1(h, i):
        lo, hi = spans[h][i]
        return rcopy(
            nc.at[pl.ds(base[h] + lo, hi - lo)], ng[h].at[pl.ds(lo, hi - lo), r_me],
            p1_s.at[h, i], p1_r.at[h, i], d_to,
        )

    def p1_local(h, i):
        lo, hi = spans[h][i]
        return pltpu.make_async_copy(
            nc.at[pl.ds(base[h] + lo, hi - lo)], ng[h].at[pl.ds(lo, hi - lo), s_o], p1_r.at[h, i]
        )

    def m_rows(w):
        return rcopy(nd.at[2 * w + 1 - c], ndt.at[w], ar_s.at[w, 0], ar_r.at[w, 0], d_c)

    @pl.when(jnp.logical_not(own_target))
    def _():
        for h in (0, 1):
            for i in (1, 0):
                p1(h, i).start()

    @pl.when(own_target)
    def _():
        for h in (0, 1):
            for i in (1, 0):
                p1_local(h, i).start()

    def p1_wait(h, i):
        @pl.when(jnp.logical_not(own_target))
        def _():
            p1(h, i).wait_recv()

        @pl.when(own_target)
        def _():
            p1_local(h, i).wait()


    def load_g(i, carry):
        g_copy(i).wait()

        @pl.when(i < chunks - STAGES + 1)
        def _():
            g_copy(i + STAGES - 1).start()

        per = 256 // ROWS
        b, r0 = i // per, (i % per) * ROWS
        for r in range(0, ROWS, 64):
            hi, lo = split2(stage[i % STAGES, r : r + 64, :])
            at = pl.ds(pl.multiple_of(r0 + r, 64), 64)
            ghi[b, at, :] = hi
            glo[b, at, :] = lo
        return carry

    def some_g(lo, hi):
        lax.fori_loop(lo, hi, load_g, 0)


    to_xp = ((0, 2, s_o), (2, 4, s_o), (2, 4, t_o), (0, 1, s_l), (2, 3, s_l), (2, 3, t_l))
    to_xm = ((0, 2, s_o), (2, 4, s_o), (2, 4, t_o), (1, 2, s_r), (3, 4, s_r), (3, 4, t_r))
    to_z = ((0, 2, s_o), (2, 4, s_o), (0, 2, s_l), (0, 2, s_r), (0, 1, s_f), (1, 2, s_f))
    of_xm = ((0, 2, s_l), (2, 4, s_l), (2, 4, t_l), (0, 1, s_f), (2, 3, s_f), (2, 3, t_f))
    of_xp = ((0, 2, s_r), (2, 4, s_r), (2, 4, t_r), (1, 2, s_f), (3, 4, s_f), (3, 4, t_f))
    of_z = ((0, 2, t_o), (2, 4, t_o), (0, 2, t_l), (0, 2, t_r), (0, 1, t_f), (1, 2, t_f))
    order = (s_o, s_l, s_r, t_o, s_f, t_l, t_r, t_f)

    def go(h, table, sems, d, i):
        lo, hi, s = table[i]
        lo, hi = cuts[h][lo], cuts[h][hi]
        blocks = ng[h].at[pl.ds(lo, hi - lo), s]
        return rcopy(blocks, blocks, sems[0].at[h, i], sems[1].at[h, i], d)

    xps, xms, zs = (xp_s, xp_r), (xm_s, xm_r), (z_s, z_r)

    def twin(h, i, s):
        blocks = ng[h].at[:, s]
        return rcopy(blocks, blocks, c_s.at[h, i], c_r.at[h, i], d_c)

    def gather_steps(h):
        def send(*what):
            for name, i in what:
                if name == "xp":
                    go(h, to_xp, xps, d_xp, i).start()
                elif name == "xm":
                    go(h, to_xm, xms, d_xm, i).start()
                elif name == "z":
                    go(h, to_z, zs, d_zn, i).start()
                else:
                    twin(h, i, order[i]).start()

        def got(*what):
            for name, i in what:
                if name == "xm":
                    go(h, of_xm, xps, d_xp, i).wait_recv()
                elif name == "xp":
                    go(h, of_xp, xms, d_xm, i).wait_recv()
                else:
                    go(h, of_z, zs, d_zn, i).wait_recv()

        def first():
            p1_wait(h, 1)
            send(("xp", 1), ("xm", 1), ("z", 1))

        def second():
            p1_wait(h, 0)
            send(("xp", 0), ("xm", 0), ("z", 0), ("c", 0))

        def b_sides():
            got(("xm", 1))
            send(("xp", 4))
            got(("xp", 1))
            send(("xm", 4))

        def b_pair():
            got(("z", 1))
            send(("xp", 2), ("xm", 2))

        def a_sides():
            got(("xm", 0))
            send(("xp", 3), ("z", 2), ("c", 1))
            got(("xp", 0))
            send(("xm", 3), ("z", 3), ("c", 2))

        def a_pair():
            got(("z", 0))
            send(("c", 3))

        def pair_sides():
            got(("xm", 2))
            send(("xp", 5))
            got(("xp", 2))
            send(("xm", 5))

        def far():
            got(("xm", 4), ("xp", 4), ("xm", 3))
            send(("z", 4))
            got(("xp", 3))
            send(("z", 5), ("c", 4))

        def last_sides():
            got(("z", 2))
            send(("c", 5))
            got(("z", 3))
            send(("c", 6))

        def last_far():
            got(("xm", 5), ("xp", 5), ("z", 4), ("z", 5))
            send(("c", 7))

        return (
            first, second, b_sides, b_pair, a_sides, a_pair, pair_sides, far, last_sides, last_far,
        )

    def spread(h):
        for i in range(8):
            twin(h, i, order[i] + 1 - 2 * c).wait_recv()

        def block(i, carry):
            p, t = i // 6, i % 6
            w = tab[2, i]
            v = ng0[jnp.clip(w, 0, FIRST - 1)].reshape(256, 256)
            if h == 1:
                late = ng1[jnp.clip(w - FIRST, 0, KEEP - FIRST - 1)].reshape(256, 256)
                v = jnp.where(w >= FIRST, late, v)
            v = jnp.where(w >= 0, v, 0.0)
            hi, lo = split2(v)
            nhi[p, t] = hi
            nlo[p, t] = lo
            return carry

        lax.fori_loop(12 * h, 12 * h + 12, block, 0)


    rounds = KEEP // QR
    early = KEEP // 3 // QR

    def product(q):
        s, p = tab[0, q], tab[1, q]
        bh = nhi[p].reshape(1536, 256)
        v = jnp.dot(ghi[s], bh, preferred_element_type=F32)
        v += jnp.dot(ghi[s], nlo[p].reshape(1536, 256), preferred_element_type=F32)
        v += jnp.dot(glo[s], bh, preferred_element_type=F32)
        pb[q] = v.reshape(4, 2, 2, 16, 256)

    def m_core(g):
        qs = pl.ds(g * QR, QR)
        return rcopy(pb.at[qs, :, :, 1 - c], rc.at[qs], rs_s.at[0, g], rs_r.at[0, g], d_c)

    def m_a(g):
        qs = pl.ds(g * QR, QR)
        return rcopy(pb.at[qs, yf, 0, c], ra.at[qs], rs_s.at[1, g], rs_r.at[1, g], d_yp)

    def m_b(g):
        qs = pl.ds(g * QR, QR)
        return rcopy(pb.at[qs, yf, 1, c], rb.at[qs], rs_s.at[2, g], rs_r.at[2, g], d_ym)

    def m_p(g):
        qs = pl.ds(g * QR, QR)
        return rcopy(pb.at[qs, yp, :, c], rp.at[qs], rs_s.at[3, g], rs_r.at[3, g], d_yp)

    def m_m(g):
        qs = pl.ds(g * QR, QR)
        return rcopy(pb.at[qs, ym, :, c], rm.at[qs], rs_s.at[4, g], rs_r.at[4, g], d_ym)

    def m_z(g):
        qs = pl.ds(g * QR, QR)
        return rcopy(pb.at[qs, y, 1 - zh, c], rz.at[qs], rs_s.at[5, g], rs_r.at[5, g], d_z2)

    ready = FIRST // QR

    def m_out(g, late):
        qs = pl.ds(g * QR, QR)
        dst = outx1.at[pl.ds(g * QR - FIRST, QR)] if late else outx0.at[qs]
        return rcopy(out.at[qs], dst, rs_s.at[6, g], rs_r.at[6, g], d_c)


    def m_down(n, w):
        return rcopy(
            dw.at[w, (at[0] + n) % 4], e1.at[w, n - 1], ar_s.at[w, n], ar_r.at[w, n], peer(n, 0, 0)
        )

    def m_plane(n2, n3, w):
        k = n2 * 4 + n3
        return rcopy(
            dw.at[w, at[0], (at[1] + n2) % 4, (at[2] + n3) % 4], e2.at[w, k - 1],
            ar_s.at[w, 3 + k], ar_r.at[w, 3 + k], peer(0, n2, n3),
        )

    def m_plane_up(n2, n3, w):
        k = n2 * 4 + n3
        part = dsum.at[w, c, at[0], at[1], at[2]]
        return rcopy(part, part, ar_s.at[w, 18 + k], ar_r.at[w, 18 + k], peer(0, n2, n3))

    def m_up(n, w):
        part = dsum.at[w, c, at[0]]
        return rcopy(part, part, ar_s.at[w, 33 + n], ar_r.at[w, 33 + n], peer(n, 0, 0))

    def m_twin(n, w):
        part = dsum.at[w, c, (at[0] + 4 - n) % 4]
        return rcopy(part, part, ar_s.at[w, 37 + n], ar_r.at[w, 37 + n], d_c)

    def term(a, b):
        return lax.dot_general(
            a.reshape(192, 256), b.reshape(192, 256), (((0,), (0,)), ((), ())),
            precision=lax.Precision.HIGHEST, preferred_element_type=F32,
        )

    def diag_steps(w):
        def terms():
            @pl.loop(ready if w else 0, rounds if w else ready)
            def _(g):
                m_out(g, w).wait_recv()

            m_rows(w).wait_recv()
            for p in (2 * w, 2 * w + 1):
                for s in range(12):
                    v = tab[3, p * 12 + s]
                    pid[p, s] = jnp.where(v >= 0, out[jnp.maximum(v, 0)], 0.0)
            p = 2 * w + c
            for s in range(12):
                v = tab[3, p * 12 + s]
                row = outx0[jnp.clip(v, 0, FIRST - 1)]
                if w:
                    more = outx1[jnp.clip(v - FIRST, 0, KEEP - FIRST - 1)]
                    row = jnp.where(v >= FIRST, more, row)
                pt[s] = jnp.where(v >= 0, row, 0.0)
            d = term(nd[p], pid[p]) + term(ndt[w], pt[...])
            dw[w, 0:2] = d[:, :128].reshape(2, 4, 4, 8, 128)
            dw[w, 2:4] = d[:, 128:].reshape(2, 4, 4, 8, 128)
            for n in (1, 3, 2):
                m_down(n, w).start()

        def after_down():
            for n in (1, 3, 2):
                m_down(n, w).wait_recv()
            dw[w, at[0]] = dw[w, at[0]] + (e1[w, 0] + e1[w, 1] + e1[w, 2])
            for n in plane:
                m_plane(*n, w).start()

        def after_plane():
            for n in plane:
                m_plane(*n, w).wait_recv()
            total = dw[w, at[0], at[1], at[2]]
            for k in range(15):
                total = total + e2[w, k]
            mine = jnp.where(at[0] < 2, gv[w, :, :128], gv[w, :, 128:])
            dsum[w, c, at[0], at[1], at[2]] = mine - total
            for n in plane:
                m_plane_up(*n, w).start()

        def after_plane_up():
            for n in plane:
                m_plane_up(*n, w).wait_recv()
            for n in (1, 3, 2):
                m_up(n, w).start()
            m_twin(0, w).start()

        def after_up():
            for n in (1, 3, 2):
                m_up(n, w).wait_recv()
                m_twin(n, w).start()

        def done():
            for n in range(4):
                m_twin(n, w).wait_recv()
            for cc in (0, 1):
                dout[2 * w + cc, :, :, :, :, 0:128] = dsum[w, cc, 0:2]
                dout[2 * w + cc, :, :, :, :, 128:256] = dsum[w, cc, 2:4]

        return terms, after_down, after_plane, after_plane_up, after_up, done

    def diagonal_sent():
        for w in (0, 1):
            m_rows(w).wait_send()
            for n in (1, 2, 3):
                m_down(n, w).wait_send()
                m_up(n, w).wait_send()
            for n in plane:
                m_plane(*n, w).wait_send()
                m_plane_up(*n, w).wait_send()
            for n in range(4):
                m_twin(n, w).wait_send()


    one, two = gather_steps(0), gather_steps(1)
    for w in (0, 1):
        m_rows(w).start()
    some_g(0, G_FIRST)
    one[0]()
    some_g(G_FIRST, G_FIRST + 2)
    one[1]()
    left = chunks - G_FIRST - 2
    for n in range(2, 7):
        some_g(G_FIRST + 2 + left * (n - 2) // 5, G_FIRST + 2 + left * (n - 1) // 5)
        one[n]()
    two[0]()
    two[1]()
    for n in range(7, 10):
        one[n]()
    spread(0)

    under = {}
    for n, r in zip(range(2, 10), GATHER_AT):
        under.setdefault(r, []).append(two[n])
    under.setdefault(early, []).append(lambda: spread(1))
    diag0, diag1 = diag_steps(0), diag_steps(1)
    inside = DIAG_AT[: sum(r < LAGS[3] + rounds for r in DIAG_AT)]
    under_late = {}
    for n, r in enumerate(inside):
        under_late.setdefault(r, []).append(diag0[n])

    def step(i, carry):
        for r, acts in under.items():

            @pl.when(i == r)
            def _(acts=acts):
                for act in acts:
                    act()

        @pl.when(i < rounds)
        def _():
            @pl.loop(0, QR)
            def _(n):
                product(i * QR + n)

            m_core(i).start()

        @pl.when((i >= LAGS[0]) & (i < rounds + LAGS[0]))
        def _():
            g = i - LAGS[0]
            m_core(g).wait_recv()

            @pl.loop(0, QR)
            def _(n):
                q = g * QR + n
                pb[q, :, :, c] += rc[q]

            m_a(g).start()
            m_b(g).start()

        @pl.when((i >= LAGS[1]) & (i < rounds + LAGS[1]))
        def _():
            g = i - LAGS[1]
            m_a(g).wait_recv()
            m_b(g).wait_recv()

            @pl.loop(0, QR)
            def _(n):
                q = g * QR + n
                pb[q, yp, 0, c] += ra[q]
                pb[q, ym, 1, c] += rb[q]

            m_p(g).start()
            m_m(g).start()

        @pl.when((i >= LAGS[2]) & (i < rounds + LAGS[2]))
        def _():
            g = i - LAGS[2]
            m_p(g).wait_recv()
            m_m(g).wait_recv()

            @pl.loop(0, QR)
            def _(n):
                q = g * QR + n
                pb[q, y, :, c] += rp[q] + rm[q]

            m_z(g).start()

        @pl.when(i >= LAGS[3])
        def _():
            g = i - LAGS[3]
            m_z(g).wait_recv()

            @pl.loop(0, QR)
            def _(n):
                q = g * QR + n
                out[q] = -(pb[q, y, zh, c] + rz[q])

            @pl.when(g < ready)
            def _():
                m_out(g, False).start()

            @pl.when(g >= ready)
            def _():
                m_out(g, True).start()

        for r, acts in under_late.items():

            @pl.when(i == r)
            def _(acts=acts):
                for act in acts:
                    act()

        return carry

    lax.fori_loop(0, rounds + LAGS[3], step, 0)
    rest = list(diag0[len(inside) :])
    for act in diag1:
        act()
        if rest:
            rest.pop(0)()

    @pl.when(jnp.logical_not(own_target))
    def _():
        for h in (0, 1):
            p1(h, 0).wait_send()
            p1(h, 1).wait_send()

    for h in (0, 1):
        for i in range(6):
            go(h, to_xp, xps, d_xp, i).wait_send()
            go(h, to_xm, xms, d_xm, i).wait_send()
            go(h, to_z, zs, d_zn, i).wait_send()
        for i in range(8):
            twin(h, i, order[i]).wait_send()

    @pl.loop(0, rounds)
    def _(g):
        m_core(g).wait_send()
        m_a(g).wait_send()
        m_b(g).wait_send()
        m_p(g).wait_send()
        m_m(g).wait_send()
        m_z(g).wait_send()

    @pl.loop(0, ready)
    def _(g):
        m_out(g, False).wait_send()

    @pl.loop(ready, rounds)
    def _(g):
        m_out(g, True).wait_send()

    diagonal_sent()


def results_kernel(a, b, a_out, b_out, a_mid, b_mid, sem_in, sem_out):
    parts = [
        (src.at[p], mid.at[p], dst.at[p], 4 * n + p)
        for p in range(4)
        for n, (src, mid, dst) in enumerate(((a, a_mid, a_out), (b, b_mid, b_out)))
    ]
    first = [pltpu.make_async_copy(src, mid, sem_in.at[k]) for src, mid, _, k in parts]
    second = [pltpu.make_async_copy(mid, dst, sem_out.at[k]) for _, mid, dst, k in parts]
    for cp in first:
        cp.start()
    for came, goes in zip(first, second):
        came.wait()
        goes.start()
    for cp in second:
        cp.wait()


VM = pl.BlockSpec(memory_space=pltpu.VMEM)
SM = pl.BlockSpec(memory_space=pltpu.SMEM)
ANY = pl.BlockSpec(memory_space=pl.ANY)
DMA = pltpu.SemaphoreType.DMA
G_FIRST = 10
DIAG_AT = (20,)
GATHER_AT = (1, 2, 3, 3, 4, 5, 5, 6)


def on_device(
    inverse_matrix, factor_blocks, factor_inverse, diag_given, block_lists, list_mask, slot_of_block
):
    k = lax.axis_index("prow")
    j = lax.axis_index("pcol")
    valid = valid_slots(block_lists, list_mask, slot_of_block)
    pos_row, idx = packed_order(valid, k)
    pos_col, _ = packed_order(valid, j // 2)
    s_q = idx % 12
    p_q = idx // 12
    col = lax.dynamic_slice_in_dim(pos_col.reshape(4, 12), (j % 2) * 6, 6, 1).reshape(24)
    tab = jnp.stack(
        [jnp.pad(s_q, (0, 12)), jnp.pad(p_q, (0, 12)), jnp.pad(col, (0, 24)), pos_row]
    )

    rounds = KEEP // QR
    results = pl.pallas_call(
        main_kernel,
        out_shape=(
            jax.ShapeDtypeStruct((4, 12, 16, 256), F32),
            jax.ShapeDtypeStruct((4, 2, 4, 4, 8, 256), F32),
        ),
        in_specs=[SM, ANY, ANY, ANY, ANY],
        out_specs=(VM, VM),
        scratch_shapes=[
            pltpu.VMEM((4, 12, 16, 256), F32),
            pltpu.VMEM((4, 256, 256), F32),
            pltpu.VMEM((KEEP, 16, 256), F32),
            pltpu.VMEM((2, 8, 256), F32),
            pltpu.VMEM((KEEP, 16, 256), F32),
            pltpu.VMEM((12, 256, 1536), BF16),
            pltpu.VMEM((12, 256, 1536), BF16),
            pltpu.VMEM((STAGES, ROWS, 1536), F32),
            pltpu.VMEM((FIRST, 16, 16, 256), F32),
            pltpu.VMEM((KEEP - FIRST, 16, 16, 256), F32),
            pltpu.VMEM((4, 6, 256, 256), BF16),
            pltpu.VMEM((4, 6, 256, 256), BF16),
            pltpu.VMEM((KEEP, 4, 2, 2, 16, 256), F32),
            pltpu.VMEM((KEEP, 4, 2, 16, 256), F32),
            pltpu.VMEM((KEEP, 16, 256), F32),
            pltpu.VMEM((KEEP, 16, 256), F32),
            pltpu.VMEM((KEEP, 2, 16, 256), F32),
            pltpu.VMEM((KEEP, 2, 16, 256), F32),
            pltpu.VMEM((KEEP, 16, 256), F32),
            pltpu.VMEM((FIRST, 16, 256), F32),
            pltpu.VMEM((KEEP - FIRST, 16, 256), F32),
            pltpu.VMEM((2, 12, 16, 256), F32),
            pltpu.VMEM((12, 16, 256), F32),
            pltpu.VMEM((2, 4, 4, 4, 8, 128), F32),
            pltpu.VMEM((2, 2, 4, 4, 4, 8, 128), F32),
            pltpu.VMEM((2, 3, 4, 4, 8, 128), F32),
            pltpu.VMEM((2, 15, 8, 128), F32),
            DMA((4,)),
            DMA((STAGES,)),
            DMA((2, 2)),
            DMA((2, 2)),
            DMA((2, 6)),
            DMA((2, 6)),
            DMA((2, 6)),
            DMA((2, 6)),
            DMA((2, 6)),
            DMA((2, 6)),
            DMA((2, 8)),
            DMA((2, 8)),
            DMA((7, rounds)),
            DMA((7, rounds)),
            DMA((2, 41)),
            DMA((2, 41)),
        ],
        compiler_params=pltpu.CompilerParams(
            collective_id=0, has_side_effects=True, vmem_limit_bytes=67043328
        ),
        name="window",
    )(tab, inverse_matrix, factor_blocks, factor_inverse, diag_given.reshape(4, 2, 4, 4, 8, 256))
    panel_inverse, diag = pl.pallas_call(
        results_kernel,
        out_shape=tuple(jax.ShapeDtypeStruct(v.shape, F32) for v in results),
        in_specs=[ANY, ANY],
        out_specs=(ANY, ANY),
        scratch_shapes=[pltpu.VMEM(v.shape, F32) for v in results] + [DMA((8,)), DMA((8,))],
        name="results",
    )(*results)
    return (panel_inverse, diag.reshape(4, 256, 256))


def solution(mesh):
    return jax.shard_map(
        on_device,
        mesh=mesh,
        in_specs=(P("prow", "pcol"), P(None, "prow", "pcol", None), P(), P(), P(), P(), P()),
        out_specs=(P(None, "prow", "pcol", None), P()),
        check_vma=False,
    )
```

```python
import functools

import jax
import jax.numpy as jnp
from jax import lax
from jax.experimental import pallas as pl
from jax.experimental.pallas import tpu as pltpu
from jax.sharding import PartitionSpec as P

MESH = pl.DeviceIdType.MESH
F32 = jnp.float32
BF16 = jnp.bfloat16
KEEP = 36
FIRST = 24
QR = 2
STAGES = 3
ROWS = 128
LAGS = (1, 3, 5, 7)


def coords():
    k = lax.axis_index("prow")
    j = lax.axis_index("pcol")
    return k // 2, j // 4, (j // 2) % 2, k % 2, j % 2


def dev(x, y, zh, zl, c):
    return (x * 2 + zl, (y * 2 + zh) * 2 + c)


def split2(v):
    hi = v.astype(BF16)
    lo = (v - hi.astype(F32)).astype(BF16)
    return hi, lo


def dot3(a, b, dim):
    (ah, al), (bh, bl) = split2(a), split2(b)
    dims = (((dim,), (0,)), ((), ()))
    out = lax.dot_general(ah, bh, dims, preferred_element_type=F32)
    out += lax.dot_general(ah, bl, dims, preferred_element_type=F32)
    return out + lax.dot_general(al, bh, dims, preferred_element_type=F32)


def valid_slots(block_lists, list_mask, slot_of_block):
    window_blocks = block_lists.shape[1]
    block_ids = jnp.arange(window_blocks, dtype=jnp.int32)
    chosen = (block_lists[:, :, None] == block_ids[None, None, :]).astype(jnp.int32)
    slot_ids = jnp.sum(chosen * slot_of_block[None, None, :], axis=2)
    matches = (slot_ids[:, :, None] == block_ids[None, None, :]).astype(jnp.int32) * list_mask[
        :, :, None
    ]
    return jnp.sum(matches, axis=1)


def packed_order(valid, group):
    v = lax.dynamic_slice_in_dim(valid, group * 12, 12, 1).reshape(48)
    i = jnp.arange(48, dtype=jnp.int32)
    pos = jnp.sum(v[None, :] * (i[None, :] < i[:, None]).astype(jnp.int32), axis=1)
    q = jnp.arange(KEEP, dtype=jnp.int32)
    hit = (pos[None, :] == q[:, None]).astype(jnp.int32) * v[None, :]
    idx = jnp.sum(hit * i[None, :], axis=1)
    return jnp.where(v > 0, pos, -1), idx


def main_kernel(
    tab, g_hbm, f_hbm, inv_hbm, given, pid, dout,
    nd, inv, nc, gv, out, ghi, glo, stage, ng0, ng1, nhi, nlo, pb, rc, ra, rb, rp, rm, rz, outx0, outx1, ndt, pt, dw, dsum, e1, e2,
    in_sem, g_sem, p1_s, p1_r, xp_s, xp_r, xm_s, xm_r, z_s, z_r, c_s, c_r, rs_s, rs_r, ar_s, ar_r,
):
    x, y, zh, zl, c = coords()
    z = 2 * zh + zl
    xp, xm, xf = (x + 1) % 4, (x + 3) % 4, (x + 2) % 4
    yp, ym, yf = (y + 1) % 4, (y + 3) % 4, (y + 2) % 4
    zn = 1 - zl
    d_xp, d_xm = dev(xp, y, zh, zl, c), dev(xm, y, zh, zl, c)
    d_zn, d_c = dev(x, y, zh, zn, c), dev(x, y, zh, zl, 1 - c)
    d_yp, d_ym = dev(x, yp, zh, zl, c), dev(x, ym, zh, zl, c)
    d_z2 = dev(x, y, 1 - zh, zl, c)
    d_to = dev((y + 2 * (x % 2)) % 4, x, zl, zh, c)
    d_from = dev(y, (x + 2 * (y % 2)) % 4, zl, zh, c)
    own_target = ((x == y) & (x % 2 == 0)) & (zl == zh)

    at = (jnp.where(c == 0, x, y), jnp.where(c == 0, y, x), z)

    def peer(n1, n2, n3):
        a, b, e = (at[0] + n1) % 4, (at[1] + n2) % 4, (at[2] + n3) % 4
        return dev(jnp.where(c == 0, a, b), jnp.where(c == 0, b, a), e // 2, e % 2, c)

    plane = [(n2, n3) for n2 in range(4) for n3 in range(4) if (n2, n3) != (0, 0)]

    barrier = pltpu.get_barrier_semaphore()
    for d in [d_c] + [peer(n, 0, 0) for n in (1, 2, 3)] + [peer(0, *n) for n in plane]:
        pl.semaphore_signal(barrier, inc=1, device_id=d, device_id_type=MESH)

    @pl.when(jnp.logical_not(own_target))
    def _():
        for d in (d_to, d_from):
            pl.semaphore_signal(barrier, inc=1, device_id=d, device_id_type=MESH)

    ins = (
        pltpu.make_async_copy(f_hbm, nd, in_sem.at[0]),
        pltpu.make_async_copy(inv_hbm, inv, in_sem.at[1]),
        pltpu.make_async_copy(given.at[c, at[0] % 2, at[1], at[2]], gv.at[0], in_sem.at[2]),
        pltpu.make_async_copy(given.at[2 + c, at[0] % 2, at[1], at[2]], gv.at[1], in_sem.at[3]),
    )
    for cp in ins:
        cp.start()

    chunks = 3072 // ROWS

    def g_copy(i):
        slot = i % STAGES
        return pltpu.make_async_copy(
            g_hbm.at[pl.ds(i * ROWS, ROWS), :], stage.at[slot], g_sem.at[slot]
        )

    for n in range(STAGES - 1):
        g_copy(n).start()

    for cp in ins:
        cp.wait()
    for p in range(4):
        nd[p] = dot3(nd[p].reshape(192, 256), inv[p], 1).reshape(12, 16, 256)

    @pl.loop(0, KEEP)
    def _(q):
        nc[q] = nd[tab[1, q], tab[0, q]]

    @pl.when(jnp.logical_not(own_target))
    def _():
        pl.semaphore_wait(barrier, 21)

    @pl.when(own_target)
    def _():
        pl.semaphore_wait(barrier, 19)

    def share(xx, zz):
        return 2 * (2 * ((xx + 2 * (y % 2)) % 4) + zz) + c

    r_me = (y * 2 + zh) * 2 + c
    s_o, s_l, s_r, s_f = (share(v, zl) for v in (x, xm, xp, xf))
    t_o, t_l, t_r, t_f = (share(v, zn) for v in (x, xm, xp, xf))
    cuts = ((0, 5, 10, 17, 24), (0, 3, 6, 9, 12))
    ng = (ng0, ng1)
    base = (0, FIRST)

    def rcopy(src, dst, ss, rs, d):
        return pltpu.make_async_remote_copy(
            src_ref=src, dst_ref=dst, send_sem=ss, recv_sem=rs, device_id=d, device_id_type=MESH
        )


    spans = tuple(((v[0], v[2]), (v[2], v[4])) for v in cuts)

    def p1(h, i):
        lo, hi = spans[h][i]
        return rcopy(
            nc.at[pl.ds(base[h] + lo, hi - lo)], ng[h].at[pl.ds(lo, hi - lo), r_me],
            p1_s.at[h, i], p1_r.at[h, i], d_to,
        )

    def p1_local(h, i):
        lo, hi = spans[h][i]
        return pltpu.make_async_copy(
            nc.at[pl.ds(base[h] + lo, hi - lo)], ng[h].at[pl.ds(lo, hi - lo), s_o], p1_r.at[h, i]
        )

    def m_rows(w):
        return rcopy(nd.at[2 * w + 1 - c], ndt.at[w], ar_s.at[w, 0], ar_r.at[w, 0], d_c)

    @pl.when(jnp.logical_not(own_target))
    def _():
        for h in (0, 1):
            for i in (1, 0):
                p1(h, i).start()

    @pl.when(own_target)
    def _():
        for h in (0, 1):
            for i in (1, 0):
                p1_local(h, i).start()

    def p1_wait(h, i):
        @pl.when(jnp.logical_not(own_target))
        def _():
            p1(h, i).wait_recv()

        @pl.when(own_target)
        def _():
            p1_local(h, i).wait()


    def load_g(i, carry):
        g_copy(i).wait()

        @pl.when(i < chunks - STAGES + 1)
        def _():
            g_copy(i + STAGES - 1).start()

        per = 256 // ROWS
        b, r0 = i // per, (i % per) * ROWS
        for r in range(0, ROWS, 64):
            hi, lo = split2(stage[i % STAGES, r : r + 64, :])
            at = pl.ds(pl.multiple_of(r0 + r, 64), 64)
            ghi[b, at, :] = hi
            glo[b, at, :] = lo
        return carry

    def some_g(lo, hi):
        lax.fori_loop(lo, hi, load_g, 0)


    to_xp = ((0, 2, s_o), (2, 4, s_o), (2, 4, t_o), (0, 1, s_l), (2, 3, s_l), (2, 3, t_l))
    to_xm = ((0, 2, s_o), (2, 4, s_o), (2, 4, t_o), (1, 2, s_r), (3, 4, s_r), (3, 4, t_r))
    to_z = ((0, 2, s_o), (2, 4, s_o), (0, 2, s_l), (0, 2, s_r), (0, 1, s_f), (1, 2, s_f))
    of_xm = ((0, 2, s_l), (2, 4, s_l), (2, 4, t_l), (0, 1, s_f), (2, 3, s_f), (2, 3, t_f))
    of_xp = ((0, 2, s_r), (2, 4, s_r), (2, 4, t_r), (1, 2, s_f), (3, 4, s_f), (3, 4, t_f))
    of_z = ((0, 2, t_o), (2, 4, t_o), (0, 2, t_l), (0, 2, t_r), (0, 1, t_f), (1, 2, t_f))
    order = (s_o, s_l, s_r, t_o, s_f, t_l, t_r, t_f)

    def go(h, table, sems, d, i):
        lo, hi, s = table[i]
        lo, hi = cuts[h][lo], cuts[h][hi]
        blocks = ng[h].at[pl.ds(lo, hi - lo), s]
        return rcopy(blocks, blocks, sems[0].at[h, i], sems[1].at[h, i], d)

    xps, xms, zs = (xp_s, xp_r), (xm_s, xm_r), (z_s, z_r)

    def twin(h, i, s):
        blocks = ng[h].at[:, s]
        return rcopy(blocks, blocks, c_s.at[h, i], c_r.at[h, i], d_c)

    def gather_steps(h):
        def send(*what):
            for name, i in what:
                if name == "xp":
                    go(h, to_xp, xps, d_xp, i).start()
                elif name == "xm":
                    go(h, to_xm, xms, d_xm, i).start()
                elif name == "z":
                    go(h, to_z, zs, d_zn, i).start()
                else:
                    twin(h, i, order[i]).start()

        def got(*what):
            for name, i in what:
                if name == "xm":
                    go(h, of_xm, xps, d_xp, i).wait_recv()
                elif name == "xp":
                    go(h, of_xp, xms, d_xm, i).wait_recv()
                else:
                    go(h, of_z, zs, d_zn, i).wait_recv()

        def first():
            p1_wait(h, 1)
            send(("xp", 1), ("xm", 1), ("z", 1))

        def second():
            p1_wait(h, 0)
            send(("xp", 0), ("xm", 0), ("z", 0), ("c", 0))

        def b_sides():
            got(("xm", 1))
            send(("xp", 4))
            got(("xp", 1))
            send(("xm", 4))

        def b_pair():
            got(("z", 1))
            send(("xp", 2), ("xm", 2))

        def a_sides():
            got(("xm", 0))
            send(("xp", 3), ("z", 2), ("c", 1))
            got(("xp", 0))
            send(("xm", 3), ("z", 3), ("c", 2))

        def a_pair():
            got(("z", 0))
            send(("c", 3))

        def pair_sides():
            got(("xm", 2))
            send(("xp", 5))
            got(("xp", 2))
            send(("xm", 5))

        def far():
            got(("xm", 4), ("xp", 4), ("xm", 3))
            send(("z", 4))
            got(("xp", 3))
            send(("z", 5), ("c", 4))

        def last_sides():
            got(("z", 2))
            send(("c", 5))
            got(("z", 3))
            send(("c", 6))

        def last_far():
            got(("xm", 5), ("xp", 5), ("z", 4), ("z", 5))
            send(("c", 7))

        return (
            first, second, b_sides, b_pair, a_sides, a_pair, pair_sides, far, last_sides, last_far,
        )

    def spread(h):
        for i in range(8):
            twin(h, i, order[i] + 1 - 2 * c).wait_recv()

        def block(i, carry):
            p, t = i // 6, i % 6
            w = tab[2, i]
            v = ng0[jnp.clip(w, 0, FIRST - 1)].reshape(256, 256)
            if h == 1:
                late = ng1[jnp.clip(w - FIRST, 0, KEEP - FIRST - 1)].reshape(256, 256)
                v = jnp.where(w >= FIRST, late, v)
            v = jnp.where(w >= 0, v, 0.0)
            hi, lo = split2(v)
            nhi[p, t] = hi
            nlo[p, t] = lo
            return carry

        lax.fori_loop(12 * h, 12 * h + 12, block, 0)


    rounds = KEEP // QR
    early = KEEP // 3 // QR

    def product(q):
        s, p = tab[0, q], tab[1, q]
        bh = nhi[p].reshape(1536, 256)
        v = jnp.dot(ghi[s], bh, preferred_element_type=F32)
        v += jnp.dot(ghi[s], nlo[p].reshape(1536, 256), preferred_element_type=F32)
        v += jnp.dot(glo[s], bh, preferred_element_type=F32)
        pb[q] = v.reshape(4, 2, 2, 16, 256)

    def m_core(g):
        qs = pl.ds(g * QR, QR)
        return rcopy(pb.at[qs, :, :, 1 - c], rc.at[qs], rs_s.at[0, g], rs_r.at[0, g], d_c)

    def m_a(g):
        qs = pl.ds(g * QR, QR)
        return rcopy(pb.at[qs, yf, 0, c], ra.at[qs], rs_s.at[1, g], rs_r.at[1, g], d_yp)

    def m_b(g):
        qs = pl.ds(g * QR, QR)
        return rcopy(pb.at[qs, yf, 1, c], rb.at[qs], rs_s.at[2, g], rs_r.at[2, g], d_ym)

    def m_p(g):
        qs = pl.ds(g * QR, QR)
        return rcopy(pb.at[qs, yp, :, c], rp.at[qs], rs_s.at[3, g], rs_r.at[3, g], d_yp)

    def m_m(g):
        qs = pl.ds(g * QR, QR)
        return rcopy(pb.at[qs, ym, :, c], rm.at[qs], rs_s.at[4, g], rs_r.at[4, g], d_ym)

    def m_z(g):
        qs = pl.ds(g * QR, QR)
        return rcopy(pb.at[qs, y, 1 - zh, c], rz.at[qs], rs_s.at[5, g], rs_r.at[5, g], d_z2)

    ready = FIRST // QR

    def m_out(g, late):
        qs = pl.ds(g * QR, QR)
        dst = outx1.at[pl.ds(g * QR - FIRST, QR)] if late else outx0.at[qs]
        return rcopy(out.at[qs], dst, rs_s.at[6, g], rs_r.at[6, g], d_c)


    def m_down(n, w):
        return rcopy(
            dw.at[w, (at[0] + n) % 4], e1.at[w, n - 1], ar_s.at[w, n], ar_r.at[w, n], peer(n, 0, 0)
        )

    def m_plane(n2, n3, w):
        k = n2 * 4 + n3
        return rcopy(
            dw.at[w, at[0], (at[1] + n2) % 4, (at[2] + n3) % 4], e2.at[w, k - 1],
            ar_s.at[w, 3 + k], ar_r.at[w, 3 + k], peer(0, n2, n3),
        )

    def m_plane_up(n2, n3, w):
        k = n2 * 4 + n3
        part = dsum.at[w, c, at[0], at[1], at[2]]
        return rcopy(part, part, ar_s.at[w, 18 + k], ar_r.at[w, 18 + k], peer(0, n2, n3))

    def m_up(n, w):
        part = dsum.at[w, c, at[0]]
        return rcopy(part, part, ar_s.at[w, 33 + n], ar_r.at[w, 33 + n], peer(n, 0, 0))

    def m_twin(n, w):
        part = dsum.at[w, c, (at[0] + 4 - n) % 4]
        return rcopy(part, part, ar_s.at[w, 37 + n], ar_r.at[w, 37 + n], d_c)

    def term(a, b):
        return dot3(a.reshape(192, 256), b.reshape(192, 256), 0)

    def diag_steps(w):
        def terms():
            @pl.loop(ready if w else 0, rounds if w else ready)
            def _(g):
                m_out(g, w).wait_recv()

            m_rows(w).wait_recv()
            for p in (2 * w, 2 * w + 1):
                for s in range(12):
                    v = tab[3, p * 12 + s]
                    pid[p, s] = jnp.where(v >= 0, out[jnp.maximum(v, 0)], 0.0)
            p = 2 * w + c
            for s in range(12):
                v = tab[3, p * 12 + s]
                row = outx0[jnp.clip(v, 0, FIRST - 1)]
                if w:
                    more = outx1[jnp.clip(v - FIRST, 0, KEEP - FIRST - 1)]
                    row = jnp.where(v >= FIRST, more, row)
                pt[s] = jnp.where(v >= 0, row, 0.0)
            d = term(nd[p], pid[p]) + term(ndt[w], pt[...])
            dw[w, 0:2] = d[:, :128].reshape(2, 4, 4, 8, 128)
            dw[w, 2:4] = d[:, 128:].reshape(2, 4, 4, 8, 128)
            for n in (1, 3, 2):
                m_down(n, w).start()

        def after_down():
            for n in (1, 3, 2):
                m_down(n, w).wait_recv()
            dw[w, at[0]] = dw[w, at[0]] + (e1[w, 0] + e1[w, 1] + e1[w, 2])
            for n in plane:
                m_plane(*n, w).start()

        def after_plane():
            for n in plane:
                m_plane(*n, w).wait_recv()
            total = dw[w, at[0], at[1], at[2]]
            for k in range(15):
                total = total + e2[w, k]
            mine = jnp.where(at[0] < 2, gv[w, :, :128], gv[w, :, 128:])
            dsum[w, c, at[0], at[1], at[2]] = mine - total
            for n in plane:
                m_plane_up(*n, w).start()

        def after_plane_up():
            for n in plane:
                m_plane_up(*n, w).wait_recv()
            for n in (1, 3, 2):
                m_up(n, w).start()
            m_twin(0, w).start()

        def after_up():
            for n in (1, 3, 2):
                m_up(n, w).wait_recv()
                m_twin(n, w).start()

        def done():
            for n in range(4):
                m_twin(n, w).wait_recv()
            for cc in (0, 1):
                dout[2 * w + cc, :, :, :, :, 0:128] = dsum[w, cc, 0:2]
                dout[2 * w + cc, :, :, :, :, 128:256] = dsum[w, cc, 2:4]

        return terms, after_down, after_plane, after_plane_up, after_up, done

    def diagonal_sent():
        for w in (0, 1):
            m_rows(w).wait_send()
            for n in (1, 2, 3):
                m_down(n, w).wait_send()
                m_up(n, w).wait_send()
            for n in plane:
                m_plane(*n, w).wait_send()
                m_plane_up(*n, w).wait_send()
            for n in range(4):
                m_twin(n, w).wait_send()


    one, two = gather_steps(0), gather_steps(1)
    for w in (0, 1):
        m_rows(w).start()
    some_g(0, G_FIRST)
    one[0]()
    some_g(G_FIRST, G_FIRST + 2)
    one[1]()
    left = chunks - G_FIRST - 2
    for n in range(2, 7):
        some_g(G_FIRST + 2 + left * (n - 2) // 5, G_FIRST + 2 + left * (n - 1) // 5)
        one[n]()
    two[0]()
    two[1]()
    for n in range(7, 10):
        one[n]()
    spread(0)

    under = {}
    for n, r in zip(range(2, 10), GATHER_AT):
        under.setdefault(r, []).append(two[n])
    under.setdefault(early, []).append(lambda: spread(1))
    diag0, diag1 = diag_steps(0), diag_steps(1)
    inside = DIAG_AT[: sum(r < LAGS[3] + rounds for r in DIAG_AT)]
    under_late = {}
    for n, r in enumerate(inside):
        under_late.setdefault(r, []).append(diag0[n])

    def step(i, carry):
        for r, acts in under.items():

            @pl.when(i == r)
            def _(acts=acts):
                for act in acts:
                    act()

        @pl.when(i < rounds)
        def _():
            @pl.loop(0, QR)
            def _(n):
                product(i * QR + n)

            m_core(i).start()

        @pl.when((i >= LAGS[0]) & (i < rounds + LAGS[0]))
        def _():
            g = i - LAGS[0]
            m_core(g).wait_recv()

            @pl.loop(0, QR)
            def _(n):
                q = g * QR + n
                pb[q, :, :, c] += rc[q]

            m_a(g).start()
            m_b(g).start()

        @pl.when((i >= LAGS[1]) & (i < rounds + LAGS[1]))
        def _():
            g = i - LAGS[1]
            m_a(g).wait_recv()
            m_b(g).wait_recv()

            @pl.loop(0, QR)
            def _(n):
                q = g * QR + n
                pb[q, yp, 0, c] += ra[q]
                pb[q, ym, 1, c] += rb[q]

            m_p(g).start()
            m_m(g).start()

        @pl.when((i >= LAGS[2]) & (i < rounds + LAGS[2]))
        def _():
            g = i - LAGS[2]
            m_p(g).wait_recv()
            m_m(g).wait_recv()

            @pl.loop(0, QR)
            def _(n):
                q = g * QR + n
                pb[q, y, :, c] += rp[q] + rm[q]

            m_z(g).start()

        @pl.when(i >= LAGS[3])
        def _():
            g = i - LAGS[3]
            m_z(g).wait_recv()

            @pl.loop(0, QR)
            def _(n):
                q = g * QR + n
                out[q] = -(pb[q, y, zh, c] + rz[q])

            @pl.when(g < ready)
            def _():
                m_out(g, False).start()

            @pl.when(g >= ready)
            def _():
                m_out(g, True).start()

        for r, acts in under_late.items():

            @pl.when(i == r)
            def _(acts=acts):
                for act in acts:
                    act()

        return carry

    lax.fori_loop(0, rounds + LAGS[3], step, 0)
    rest = list(diag0[len(inside) :])
    for act in diag1:
        act()
        if rest:
            rest.pop(0)()

    @pl.when(jnp.logical_not(own_target))
    def _():
        for h in (0, 1):
            p1(h, 0).wait_send()
            p1(h, 1).wait_send()

    for h in (0, 1):
        for i in range(6):
            go(h, to_xp, xps, d_xp, i).wait_send()
            go(h, to_xm, xms, d_xm, i).wait_send()
            go(h, to_z, zs, d_zn, i).wait_send()
        for i in range(8):
            twin(h, i, order[i]).wait_send()

    @pl.loop(0, rounds)
    def _(g):
        m_core(g).wait_send()
        m_a(g).wait_send()
        m_b(g).wait_send()
        m_p(g).wait_send()
        m_m(g).wait_send()
        m_z(g).wait_send()

    @pl.loop(0, ready)
    def _(g):
        m_out(g, False).wait_send()

    @pl.loop(ready, rounds)
    def _(g):
        m_out(g, True).wait_send()

    diagonal_sent()


def results_kernel(a, b, a_out, b_out, a_mid, b_mid, sem_in, sem_out):
    parts = [
        (src.at[p], mid.at[p], dst.at[p], 4 * n + p)
        for p in range(4)
        for n, (src, mid, dst) in enumerate(((a, a_mid, a_out), (b, b_mid, b_out)))
    ]
    first = [pltpu.make_async_copy(src, mid, sem_in.at[k]) for src, mid, _, k in parts]
    second = [pltpu.make_async_copy(mid, dst, sem_out.at[k]) for _, mid, dst, k in parts]
    for cp in first:
        cp.start()
    for came, goes in zip(first, second):
        came.wait()
        goes.start()
    for cp in second:
        cp.wait()


VM = pl.BlockSpec(memory_space=pltpu.VMEM)
SM = pl.BlockSpec(memory_space=pltpu.SMEM)
ANY = pl.BlockSpec(memory_space=pl.ANY)
DMA = pltpu.SemaphoreType.DMA
G_FIRST = 10
DIAG_AT = (20,)
GATHER_AT = (1, 2, 3, 3, 4, 5, 5, 6)


def on_device(
    inverse_matrix, factor_blocks, factor_inverse, diag_given, block_lists, list_mask, slot_of_block
):
    k = lax.axis_index("prow")
    j = lax.axis_index("pcol")
    valid = valid_slots(block_lists, list_mask, slot_of_block)
    pos_row, idx = packed_order(valid, k)
    pos_col, _ = packed_order(valid, j // 2)
    s_q = idx % 12
    p_q = idx // 12
    col = lax.dynamic_slice_in_dim(pos_col.reshape(4, 12), (j % 2) * 6, 6, 1).reshape(24)
    tab = jnp.stack(
        [jnp.pad(s_q, (0, 12)), jnp.pad(p_q, (0, 12)), jnp.pad(col, (0, 24)), pos_row]
    )

    rounds = KEEP // QR
    results = pl.pallas_call(
        main_kernel,
        out_shape=(
            jax.ShapeDtypeStruct((4, 12, 16, 256), F32),
            jax.ShapeDtypeStruct((4, 2, 4, 4, 8, 256), F32),
        ),
        in_specs=[SM, ANY, ANY, ANY, ANY],
        out_specs=(VM, VM),
        scratch_shapes=[
            pltpu.VMEM((4, 12, 16, 256), F32),
            pltpu.VMEM((4, 256, 256), F32),
            pltpu.VMEM((KEEP, 16, 256), F32),
            pltpu.VMEM((2, 8, 256), F32),
            pltpu.VMEM((KEEP, 16, 256), F32),
            pltpu.VMEM((12, 256, 1536), BF16),
            pltpu.VMEM((12, 256, 1536), BF16),
            pltpu.VMEM((STAGES, ROWS, 1536), F32),
            pltpu.VMEM((FIRST, 16, 16, 256), F32),
            pltpu.VMEM((KEEP - FIRST, 16, 16, 256), F32),
            pltpu.VMEM((4, 6, 256, 256), BF16),
            pltpu.VMEM((4, 6, 256, 256), BF16),
            pltpu.VMEM((KEEP, 4, 2, 2, 16, 256), F32),
            pltpu.VMEM((KEEP, 4, 2, 16, 256), F32),
            pltpu.VMEM((KEEP, 16, 256), F32),
            pltpu.VMEM((KEEP, 16, 256), F32),
            pltpu.VMEM((KEEP, 2, 16, 256), F32),
            pltpu.VMEM((KEEP, 2, 16, 256), F32),
            pltpu.VMEM((KEEP, 16, 256), F32),
            pltpu.VMEM((FIRST, 16, 256), F32),
            pltpu.VMEM((KEEP - FIRST, 16, 256), F32),
            pltpu.VMEM((2, 12, 16, 256), F32),
            pltpu.VMEM((12, 16, 256), F32),
            pltpu.VMEM((2, 4, 4, 4, 8, 128), F32),
            pltpu.VMEM((2, 2, 4, 4, 4, 8, 128), F32),
            pltpu.VMEM((2, 3, 4, 4, 8, 128), F32),
            pltpu.VMEM((2, 15, 8, 128), F32),
            DMA((4,)),
            DMA((STAGES,)),
            DMA((2, 2)),
            DMA((2, 2)),
            DMA((2, 6)),
            DMA((2, 6)),
            DMA((2, 6)),
            DMA((2, 6)),
            DMA((2, 6)),
            DMA((2, 6)),
            DMA((2, 8)),
            DMA((2, 8)),
            DMA((7, rounds)),
            DMA((7, rounds)),
            DMA((2, 41)),
            DMA((2, 41)),
        ],
        compiler_params=pltpu.CompilerParams(
            collective_id=0, has_side_effects=True, vmem_limit_bytes=67043328
        ),
        name="window",
    )(tab, inverse_matrix, factor_blocks, factor_inverse, diag_given.reshape(4, 2, 4, 4, 8, 256))
    panel_inverse, diag = pl.pallas_call(
        results_kernel,
        out_shape=tuple(jax.ShapeDtypeStruct(v.shape, F32) for v in results),
        in_specs=[ANY, ANY],
        out_specs=(ANY, ANY),
        scratch_shapes=[pltpu.VMEM(v.shape, F32) for v in results] + [DMA((8,)), DMA((8,))],
        name="results",
    )(*results)
    return (panel_inverse, diag.reshape(4, 256, 256))


def solution(mesh):
    return jax.shard_map(
        on_device,
        mesh=mesh,
        in_specs=(P("prow", "pcol"), P(None, "prow", "pcol", None), P(), P(), P(), P(), P()),
        out_specs=(P(None, "prow", "pcol", None), P()),
        check_vma=False,
    )
```
